512 devices in a mesh: src: 16 (over z_hi, x, core), rows: 32 (over z_lo, y).
Axes of the slice: x: 4, y: 8, z: 8 (z_hi: 2, z_lo: 4; z = z_hi * 4 + z_lo), core: 2. Of those that a mesh axis runs over, the one named last changes fastest.
Arguments:
- mask_param: float32 [512, 8192], P('rows'), may hold values from -6 to 6
- target: int32 [512, 8192], P('rows', 'src'), may hold values 0 or 1
- source_weight: float32 [16], replicated, may hold values from 0.25 to 4
- row_shift: int32 [16], replicated, may hold values from -8 to 8
- col_shift: int32 [16], replicated, may hold values from -32 to 32
Outputs:
- mask_grad: float32 [512, 8192], P('rows', 'src')
The draws below stay inside these ranges and needn't reach their ends.
All inputs are finite; a program needn't handle non-finite values. No bound on the sum of `target` on one device may be relied on, other than what follows from the above.
Results may differ from the reference program's by a relative error of at most 0.0003.
Values sent between devices are 32-bit elements; how exact they have to be, the bound alone decides.
No kernel may reach another device: no remote copies, remote signals or barrier semaphores. Data moves between devices by JAX's collectives and lax.ppermute only.
A program may use at most 64 MiB of HBM per device.

```python
import math
import jax
import jax.numpy as jnp
from jax import lax

NC = 8192
NR = 512
SRC = 16
KR = 32
KC = 128


def touch_ends(result, key, least, high):
    longest = result.shape.index(max(result.shape))
    spots = []
    for shift in (0, 1):
        where = [jax.random.randint(jax.random.fold_in(key, axis), (), 0, length) for axis, length in enumerate(result.shape)]
        where[longest] = (where[longest] + shift) % result.shape[longest]
        spots.append(tuple(where))
    return result.at[spots[0]].set(least).at[spots[1]].set(high)


def shard_levels(own_key, shape, cuts, least, largest):
    level, own = 1.0, jax.random.fold_in(own_key, 6)
    for axis_at, shards_of in cuts:
        heights = jnp.exp(jax.random.uniform(jax.random.fold_in(own, axis_at), (shards_of,), jnp.float32, least / len(cuts), largest / len(cuts)))
        level = level * jnp.repeat(heights, shape[axis_at] // shards_of).reshape([-1 if axis == axis_at else 1 for axis in range(len(shape))])
    return level


def normal_values(rng, dims, scale, limit, cuts=(), kind=jnp.bfloat16):
    values = jax.random.normal(rng, dims, jnp.float32) * scale
    if len(cuts) > 0:
        values = shard_levels(rng, dims, cuts, -0.22, 0.18) * values
    return jnp.clip(values, min=-limit, max=limit).astype(kind)


def setup_inputs(seed: int = 0) -> dict:
    arg_keys = jax.random.split(jax.random.key(seed), 6)
    mask_param = normal_values(arg_keys[0], (NR, NC), 1.0, 6.0, ((0, 32),), jnp.float32)
    target = touch_ends((jax.random.randint(arg_keys[1], (NR, NC), 0, 2) < 1).astype(jnp.int32), jax.random.fold_in(arg_keys[1], 1), 0, 1)
    source_weight = jnp.clip(jnp.exp(jax.random.uniform(arg_keys[2], (SRC,), jnp.float32, math.log(0.25), math.log(4.0))), 0.25, 4.0)
    row_shift = touch_ends(jax.random.randint(arg_keys[3], (SRC,), -(KR // 4), KR // 4 + 1), jax.random.fold_in(arg_keys[3], 1), -(KR // 4), (KR // 4 + 1) - 1).astype(jnp.int32)
    col_shift = touch_ends(jax.random.randint(arg_keys[4], (SRC,), -(KC // 4), KC // 4 + 1), jax.random.fold_in(arg_keys[4], 1), -(KC // 4), (KC // 4 + 1) - 1).astype(jnp.int32)
    return dict(mask_param=mask_param, target=target, source_weight=source_weight, row_shift=row_shift, col_shift=col_shift)


steepness = 250.0
threshold_level = 0.25
loss_weight = 8.0


def centered(number):
    return jnp.arange(number, dtype=jnp.int32) - number // 2


def pupil_mask(row_offset, col_offset):
    radius_rows = KR // 4
    radius_cols = KC // 4
    row_term = (centered(KR) + row_offset) ** 2 * (radius_cols * radius_cols)
    col_term = (centered(KC) + col_offset) ** 2 * (radius_rows * radius_rows)
    limit_value = (radius_rows * radius_cols) ** 2
    return (row_term[:, None] + col_term[None, :] <= limit_value).astype(jnp.float32)


def reference(mask_param, target, source_weight, row_shift, col_shift):
    opening = jax.nn.sigmoid(mask_param)
    row_index = jnp.mod(centered(KR), NR).astype(jnp.int32)
    col_index = jnp.mod(centered(KC), NC).astype(jnp.int32)
    spectrum = jnp.fft.fft2(opening, norm="ortho")
    band_spec = spectrum[row_index][:, col_index]
    weights = source_weight / jnp.sum(source_weight)

    def spread_band(values):
        padded = jnp.zeros((NR, NC), band_spec.dtype)
        return padded.at[row_index[:, None], col_index[None, :]].set(values)

    def field_of(point_row, point_col):
        opened = band_spec * pupil_mask(point_row, point_col)
        return jnp.fft.ifft2(spread_band(opened), norm="ortho")

    def add_intensity(running, entries):
        weight, point_row, point_col = entries
        field_now = field_of(point_row, point_col)
        return running + weight * (jnp.real(field_now) ** 2 + jnp.imag(field_now) ** 2), None

    intensity = lax.scan(add_intensity, jnp.zeros((NR, NC), jnp.float32), (weights, row_shift, col_shift))[0]
    resist = jax.nn.sigmoid(steepness * (intensity - threshold_level))
    slope = 2.0 * loss_weight * (resist - target.astype(jnp.float32)) * steepness * resist * (1.0 - resist)

    def add_adjoint(running, entries):
        weight, point_row, point_col = entries
        field_now = field_of(point_row, point_col)
        cotangent = 2.0 * weight * slope * field_now
        back_band = jnp.fft.fft2(cotangent, norm="ortho")[row_index][:, col_index]
        return running + pupil_mask(point_row, point_col) * back_band, None

    adjoint = lax.scan(add_adjoint, jnp.zeros((KR, KC), band_spec.dtype), (weights, row_shift, col_shift))[0]
    grad_open = jnp.real(jnp.fft.ifft2(spread_band(adjoint), norm="ortho"))
    return (grad_open * opening * (1.0 - opening)).astype(jnp.float32)
```

```python
import math

import jax
import jax.numpy as jnp
import numpy as np
from jax import lax
from jax.sharding import PartitionSpec as P

steepness = 250.0
threshold_level = 0.25
loss_weight = 8.0
highest = lax.Precision.HIGHEST

NR = 512
NC = 8192
KR = 32
KC = 128
MC = 256
HALF = KC // 2
SHARE = 512
BLOCKS = NC // SHARE
ROWS = 16
UNIT = 1.0 / math.sqrt(NR * NC)


def dot(left, right, precision=highest):
    return jnp.dot(left, right, precision=precision, preferred_element_type=jnp.float32)


def wave(frequency, position, period):
    angle = (np.outer(frequency, position) % period) * (2.0 * np.pi / period)
    return np.cos(angle), np.sin(angle)


def f32(table):
    return np.asarray(table, dtype=np.float32)


def column_tables():
    half = np.arange(HALF)
    cos, sin = wave(np.arange(HALF + 1), np.arange(SHARE), NC)
    real, imag = cos, -sin
    first = np.concatenate([real[:HALF], real[HALF:], imag[1:HALF]])
    second = np.concatenate([imag[:HALF], imag[HALF:], real[1:HALF]])
    base = np.concatenate([first, second]).T
    order = np.concatenate([half, [HALF], half[1:]])
    sign = np.concatenate([np.ones(HALF + 1), -np.ones(HALF - 1)])
    turn_cos, turn_sin = wave(np.arange(BLOCKS), order, BLOCKS)
    return f32(base), f32(turn_cos), f32(turn_sin * sign), f32(turn_sin)


def spread_table():
    table = np.zeros((KC + 1, 2 * KC))
    for frequency in range(-HALF, HALF):
        size = abs(frequency)
        at = frequency + HALF
        table[size if size < HALF else HALF, at] = 1.0
        if size == HALF:
            table[KC, KC + at] = -1.0
        elif size > 0:
            table[HALF + size, KC + at] = 1.0 if frequency > 0 else -1.0
    return f32(table)


def row_table():
    cos, sin = wave(np.arange(KR) - KR // 2, np.arange(NR), NR)
    return f32(np.concatenate([cos, sin]))


def sample_tables():
    cos, sin = wave(np.arange(KC) - HALF, np.arange(MC), MC)
    inverse = np.block([[cos, sin], [-sin, cos]])
    return f32(inverse), f32(inverse.T)


def interpolation_table():
    size = np.arange(1, HALF + 1)
    place = (np.arange(MC)[:, None] * (NC // MC) - np.arange(SHARE)[None, :]) % NC
    total = np.ones_like(place, dtype=np.float64)
    for k in size:
        total += 2.0 * np.cos(((place * k) % NC) * (2.0 * np.pi / NC))
    return f32(total / MC)


def fold_tables():
    columns = np.zeros((KC, KC + 1))
    odd = np.zeros((KC, KC + 1))
    even = np.zeros((KC, KC + 1))
    for frequency in range(-HALF, HALF):
        at, size = frequency + HALF, abs(frequency)
        even[at, size] = 1.0
        if size > 0:
            odd[at, size - 1] = -1.0 if frequency > 0 else 1.0
    columns = np.concatenate([even[:, : HALF + 1], odd[:, :HALF]], axis=1)
    rows_even = np.zeros((KR // 2 + 1, KR))
    rows_odd = np.zeros((KR // 2 + 1, KR))
    for frequency in range(-KR // 2, KR // 2):
        at, size = frequency + KR // 2, abs(frequency)
        rows_even[size, at] = 1.0
        rows_odd[size, at] = float(np.sign(frequency))
    return f32(columns), f32(rows_even), f32(rows_odd)


def final_tables():
    cos, sin = wave(np.arange(NR), np.arange(KR // 2 + 1), NR)
    rows = np.concatenate([cos, sin], axis=1)
    cos_y, sin_y = wave(np.arange(HALF + 1), np.arange(SHARE), NC)
    columns = np.concatenate([cos_y, sin_y[1:]])
    turn_cos, turn_sin = wave(np.arange(BLOCKS), np.arange(HALF + 1), BLOCKS)
    return f32(rows), f32(columns), f32(turn_cos), f32(turn_sin)


def everywhere(values, axis, count):
    spread = jnp.broadcast_to(values[None], (count,) + values.shape)
    return lax.all_to_all(spread, axis, 0, 0, tiled=True)


def pupils(row_shift, col_shift):
    radius_rows = KR // 4
    radius_cols = KC // 4
    fr = jnp.arange(KR, dtype=jnp.int32) - KR // 2
    fc = jnp.arange(KC, dtype=jnp.int32) - HALF
    row_term = (fr[:, None] + row_shift[None, :]) ** 2 * (radius_cols * radius_cols)
    col_term = (fc[None, :] + col_shift[:, None]) ** 2 * (radius_rows * radius_rows)
    limit_value = (radius_rows * radius_cols) ** 2
    return (row_term[:, :, None] + col_term[None] <= limit_value).astype(jnp.float32)


def local(mask_param, target, source_weight, row_shift, col_shift):
    src_index = lax.axis_index("src")
    row_index = lax.axis_index("rows")
    src_count = lax.axis_size("src")
    row_count = lax.axis_size("rows")
    points = source_weight.shape[0]
    opening = jax.nn.sigmoid(mask_param)
    weights = source_weight / jnp.sum(source_weight)
    opened = pupils(row_shift, col_shift)

    base, turn_cos, turn_side, turn_sin = column_tables()
    stacked = jnp.concatenate([opening[:, SHARE * b : SHARE * (b + 1)] for b in range(BLOCKS)])
    parts = dot(stacked, base).reshape(BLOCKS, ROWS, 2 * KC)
    first, second = parts[:, :, :KC], parts[:, :, KC:]
    packed = jnp.sum(first * turn_cos[:, None] + second * turn_side[:, None], axis=0)
    edge = jnp.sum(
        second[:, :, HALF] * turn_cos[:, None, HALF] - first[:, :, HALF] * turn_sin[:, None, HALF],
        axis=0,
    )
    message = jnp.concatenate([packed, jnp.pad(edge, (0, KC - ROWS))[None]])
    heard = everywhere(message, "rows", row_count)
    column_part = jnp.concatenate(
        [heard[:, :ROWS].reshape(NR, KC), heard[:, ROWS, :ROWS].reshape(NR, 1)], axis=1
    )
    both = dot(dot(row_table() * UNIT, column_part), spread_table())
    cr, ci = both[:KR, :KC], both[:KR, KC:]
    sr, si = both[KR:, :KC], both[KR:, KC:]
    band_real, band_imag = cr + si, ci - sr

    own = lax.dynamic_slice_in_dim(jnp.asarray(row_table().T), row_index * ROWS, ROWS)
    own_cos, own_sin = own[:, :KR], own[:, KR:]
    turn = jnp.concatenate(
        [
            jnp.concatenate([own_cos, -own_sin], axis=1),
            jnp.concatenate([own_sin, own_cos], axis=1),
        ]
    )
    masked = jnp.concatenate([band_real[:, None] * opened, band_imag[:, None] * opened])
    head = dot(turn * UNIT, masked.reshape(2 * KR, points * KC)).reshape(2, ROWS, points, KC)
    head = head.transpose(2, 1, 0, 3).reshape(points * ROWS, 2 * KC)
    to_samples, from_samples = sample_tables()
    field = dot(head, to_samples).reshape(points, ROWS, 2 * MC)
    power = field[:, :, :MC] ** 2 + field[:, :, MC:] ** 2
    samples = jnp.sum(weights[:, None, None] * power, axis=0)
    step = MC // BLOCKS
    twice = jnp.concatenate([samples, samples], axis=1)
    near = lax.dynamic_slice_in_dim(twice, src_index * step, MC, 1)
    interpolate = interpolation_table()
    intensity = dot(near, interpolate)
    resist = jax.nn.sigmoid(steepness * (intensity - threshold_level))
    slope = (
        2.0
        * loss_weight
        * (resist - target.astype(jnp.float32))
        * steepness
        * resist
        * (1.0 - resist)
    )
    low = dot(slope, interpolate.T)
    twice = jnp.concatenate([low, low], axis=1)
    low = lax.dynamic_slice_in_dim(twice, (src_count - src_index) * step, MC, 1)
    low = jnp.sum(everywhere(low, "src", src_count), axis=0)

    scaled = (2.0 * UNIT * weights)[:, None, None] * jnp.concatenate([low, low], axis=1)[None]
    back = dot((scaled * field).reshape(points * ROWS, 2 * MC), from_samples)
    back = back.reshape(points, ROWS, 2, KC).transpose(2, 1, 0, 3).reshape(2 * ROWS, points * KC)
    adjoint = dot(turn.T, back).reshape(2, KR, points, KC)
    adjoint = jnp.sum(adjoint * opened[None], axis=2).reshape(2 * KR, KC)

    fold_columns, fold_even, fold_odd = fold_tables()
    folded = dot(adjoint, fold_columns)
    real_even, real_odd = folded[:KR, : HALF + 1], folded[:KR, HALF + 1 :]
    imag_even, imag_odd = folded[KR:, : HALF + 1], folded[KR:, HALF + 1 :]
    even = jnp.concatenate([dot(fold_even, real_even), -dot(fold_odd, imag_even)])
    odd = jnp.concatenate([dot(fold_even, imag_odd), dot(fold_odd, real_odd)])
    kinds = 2 * (KR // 2 + 1)
    message = jnp.concatenate(
        [
            jnp.concatenate([even[:, :HALF], odd], axis=1),
            jnp.pad(even[:, HALF], (0, KC - kinds))[None],
        ]
    )
    total = jnp.sum(everywhere(message, "rows", row_count), axis=0)
    even = jnp.concatenate([total[:kinds, :HALF], total[kinds, :kinds].reshape(kinds, 1)], axis=1)
    odd = total[:kinds, HALF:]
    rows, columns, turn_cos, turn_sin = final_tables()
    rows = lax.dynamic_slice_in_dim(jnp.asarray(rows * np.float32(UNIT)), row_index * ROWS, ROWS)
    cos_part = dot(rows, even)
    sin_part = jnp.pad(dot(rows, odd), ((0, 0), (1, 0)))
    tc = lax.dynamic_slice_in_dim(jnp.asarray(turn_cos), src_index, 1)
    ts = lax.dynamic_slice_in_dim(jnp.asarray(turn_sin), src_index, 1)
    cos_turned = cos_part * tc + sin_part * ts
    sin_turned = sin_part * tc - cos_part * ts
    grad = dot(jnp.concatenate([cos_turned, sin_turned[:, 1:]], axis=1), columns)
    own_open = lax.dynamic_slice_in_dim(opening, src_index * SHARE, SHARE, 1)
    return grad * own_open * (1.0 - own_open)


def solution(mesh):
    placed = (P("rows", None), P("rows", "src"), P(), P(), P())
    return jax.shard_map(
        local, mesh=mesh, in_specs=placed, out_specs=P("rows", "src"), check_vma=False
    )
```

```python
import math

import jax
import jax.numpy as jnp
import numpy as np
from jax import lax
from jax.experimental import pallas as pl
from jax.experimental.pallas import tpu as pltpu
from jax.sharding import Mesh
from jax.sharding import PartitionSpec as P

steepness = 250.0
threshold_level = 0.25
loss_weight = 8.0
highest = lax.Precision.HIGHEST
KERNELS = True

NR = 512
NC = 8192
KR = 32
KC = 128
MC = 256
HALF = KC // 2
SHARE = 512
BLOCKS = NC // SHARE
ROWS = 16
ROW_BLOCKS = NR // ROWS
POINTS = 16
NEAR = 8
STEP = MC // BLOCKS
UNIT = 1.0 / math.sqrt(NR * NC)


def f32(table):
    return np.ascontiguousarray(np.asarray(table, dtype=np.float32))


def wave(frequency, position, period):
    angle = (np.outer(frequency, position) % period) * (2.0 * np.pi / period)
    return np.cos(angle), np.sin(angle)


def column_table():
    cos, sin = wave(np.arange(HALF + 1), np.arange(SHARE), NC)
    table = np.zeros((2 * KC, SHARE))
    table[:HALF] = cos[:HALF]
    table[HALF] = cos[HALF]
    table[HALF + 1 : KC] = -sin[1:HALF]
    table[KC] = -sin[HALF]
    return f32(table.T)


def turn_tables():
    cos, sin = wave(np.arange(BLOCKS), np.arange(HALF), BLOCKS)
    return f32(np.concatenate([cos, cos], axis=1)), f32(np.concatenate([sin, -sin], axis=1))


def spread_table():
    table = np.zeros((KC, 2 * KC))
    for frequency in range(-HALF, HALF):
        size, at = abs(frequency), frequency + HALF
        table[size, at] = 1.0
        if 0 < size < HALF:
            table[HALF + size, KC + at] = 1.0 if frequency > 0 else -1.0
    return f32(table)


def band_tables():
    cos, sin = wave(np.arange(KR) - KR // 2, np.arange(NR), NR)
    rows = np.concatenate([cos, sin]) * (UNIT * UNIT)
    split = rows.reshape(2 * KR, ROW_BLOCKS, 2, ROWS // 2)
    edge = np.concatenate([split[:, :, 0].reshape(2 * KR, -1), split[:, :, 1].reshape(2 * KR, -1)])
    return f32(rows), f32(edge)


def own_row_table():
    cos, sin = wave(np.arange(NR), np.arange(KR) - KR // 2, NR)
    cos = cos.reshape(ROW_BLOCKS, ROWS, KR)
    sin = sin.reshape(ROW_BLOCKS, ROWS, KR)
    turn = np.concatenate(
        [np.concatenate([cos, -sin], axis=2), np.concatenate([sin, cos], axis=2)], axis=1
    )
    return f32(turn)


def sample_table():
    cos, sin = wave(np.arange(KC) - HALF, np.arange(MC), MC)
    return np.block([[cos, sin], [-sin, cos]])


def interpolation_table():
    place = (np.arange(MC)[:, None] * (NC // MC) - np.arange(SHARE)[None, :]) % NC
    total = np.ones_like(place, dtype=np.float64)
    for k in range(1, HALF + 1):
        total += 2.0 * np.cos(((place * k) % NC) * (2.0 * np.pi / NC))
    return total / MC


def fold_tables():
    columns = np.zeros((KC, 2 * KC))
    for frequency in range(-HALF, HALF):
        at, size = frequency + HALF, abs(frequency)
        columns[at, size] = 1.0
        if size > 0:
            columns[at, HALF + size] = -1.0 if frequency > 0 else 1.0
    columns[0, KC] = 1.0
    columns[0, HALF] = 1.0
    rows = np.zeros((KC, 2 * KR))
    for frequency in range(-KR // 2, KR // 2):
        at, size = frequency + KR // 2, abs(frequency)
        rows[size, at] = 1.0
        if size > 0:
            rows[KR // 2 + size, KR + at] = float(np.sign(frequency))
    pick = np.zeros((8, KC))
    pick[1, 0] = 1.0
    return f32(columns), f32(rows), f32(pick)


def final_tables():
    cos, sin = wave(np.arange(NR), np.arange(KR // 2 + 1), NR)
    rows = np.zeros((NR, KC))
    rows[:, : KR // 2 + 1] = cos * UNIT
    rows[:, KR // 2 + 1 : KR + 1] = sin[:, 1:] * UNIT
    cos_y, sin_y = wave(np.arange(HALF + 1), np.arange(SHARE), NC)
    columns = np.concatenate([cos_y, sin_y[1:HALF]])
    return f32(rows.reshape(ROW_BLOCKS, ROWS, KC)), f32(columns), f32(sin_y[HALF:])


def dot(left, right):
    return jnp.dot(left, right, precision=highest, preferred_element_type=jnp.float32)


def dot_nt(left, right, precision=highest):
    return lax.dot_general(
        left, right, (((1,), (1,)), ((), ())), precision=precision, preferred_element_type=jnp.float32
    )


def split(values):
    high = values.astype(jnp.bfloat16)
    return high, (values - high.astype(jnp.float32)).astype(jnp.bfloat16)


def dot3_nt(left, right):
    high, low = split(left)
    right_high, right_low = split(right)
    one = lambda a, b: dot_nt(a, b, None)
    return one(high, right_high) + (one(high, right_low) + one(low, right_high))


def dot_tn(left, right):
    return lax.dot_general(
        left, right, (((0,), (0,)), ((), ())), precision=highest, preferred_element_type=jnp.float32
    )


def logistic(values):
    return 1.0 / (1.0 + jnp.exp(-values))


def roll(values, shift):
    if KERNELS:
        return pltpu.roll(values, shift, axis=1)
    return jnp.roll(values, shift, axis=1)


def lanes(shape):
    return lax.broadcasted_iota(jnp.int32, shape, 1)


def columns_math(mask, base, turn_cos, turn_sin):
    stacked = jnp.concatenate(
        [logistic(mask[:, SHARE * b : SHARE * (b + 1)]) for b in range(BLOCKS)], axis=0
    )
    parts = dot(stacked, base)
    main = jnp.zeros((ROWS, KC), jnp.float32)
    edge = jnp.zeros((ROWS, KC), jnp.float32)
    for b in range(BLOCKS):
        part = parts[ROWS * b : ROWS * (b + 1)]
        first = part[:, :KC]
        main = main + first * turn_cos[b : b + 1] + roll(first, HALF) * turn_sin[b : b + 1]
        edge = edge + part[:, KC:]
    return jnp.concatenate([main, edge[:8] + roll(edge[8:], 1)], axis=0)


def pupil(row_shift, col_shift):
    radius_rows = KR // 4
    radius_cols = KC // 4
    fr = lax.broadcasted_iota(jnp.int32, (KR, KC), 0) - KR // 2 + row_shift
    fc = lanes((KR, KC)) - HALF + col_shift
    limit_value = (radius_rows * radius_cols) ** 2
    inside = fr * fr * (radius_cols * radius_cols) + fc * fc * (radius_rows * radius_rows)
    return (inside <= limit_value).astype(jnp.float32)


def middle_math(
    half,
    weight,
    row_shift,
    col_shift,
    heard,
    target,
    turn,
    rows,
    rows_edge,
    spread,
    to_samples,
    interpolate,
    fold_columns,
    fold_rows,
    pick,
):
    main = jnp.concatenate([heard[b, :ROWS] for b in range(ROW_BLOCKS)], axis=0)
    edge = jnp.concatenate([heard[b, ROWS:] for b in range(ROW_BLOCKS)], axis=0)
    both = dot(dot(rows, main), spread)
    edges = dot(rows_edge, edge)
    edge_column = edges[: 2 * KR, 0:1] + edges[2 * KR :, 1:2]
    real = both[:, :KC]
    imag = both[:, KC:] - jnp.where(lanes((2 * KR, KC)) == 0, edge_column, 0.0)
    band_real = real[:KR] + imag[KR:]
    band_imag = imag[:KR] - real[KR:]

    opened = [pupil(row_shift[s], col_shift[s]) for s in range(POINTS)]
    masked = jnp.concatenate(
        [
            jnp.concatenate([band_real * opened[s], band_imag * opened[s]], axis=0)
            for s in range(POINTS)
        ],
        axis=1,
    )
    head = dot(turn, masked)
    head = jnp.concatenate(
        [
            jnp.concatenate(
                [head[:ROWS, KC * s : KC * (s + 1)], head[ROWS:, KC * s : KC * (s + 1)]], axis=1
            )
            for s in range(POINTS)
        ],
        axis=0,
    )
    field = dot(head, to_samples)
    samples = jnp.zeros((ROWS, MC), jnp.float32)
    total = 0.0
    for s in range(POINTS):
        now = field[ROWS * s : ROWS * (s + 1)]
        samples = samples + weight[s] * (now[:, :MC] * now[:, :MC] + now[:, MC:] * now[:, MC:])
        total = total + weight[s]
    share = 1.0 / jnp.full((ROWS, MC), total, jnp.float32)
    samples = samples * share
    samples = jnp.where(half == 1, roll(samples, MC // 2), samples)
    near = jnp.concatenate([samples] + [roll(samples, MC - STEP * j) for j in range(1, NEAR)], axis=0)
    intensity = dot(near, interpolate)
    resist = logistic(steepness * (intensity - threshold_level))
    slope = (
        2.0
        * loss_weight
        * (resist - target.astype(jnp.float32))
        * steepness
        * resist
        * (1.0 - resist)
    )
    lows = dot3_nt(slope, interpolate)
    low = lows[:ROWS]
    for j in range(1, NEAR):
        low = low + roll(lows[ROWS * j : ROWS * (j + 1)], STEP * j)
    low = jnp.where(half == 1, roll(low, MC // 2), low)
    low = low * share * (2.0 * UNIT)
    wide = jnp.concatenate([low, low], axis=1)
    scaled = jnp.concatenate(
        [(weight[s] * wide) * field[ROWS * s : ROWS * (s + 1)] for s in range(POINTS)], axis=0
    )
    back = dot3_nt(scaled, to_samples)
    back = jnp.concatenate(
        [
            jnp.concatenate(
                [back[ROWS * s : ROWS * (s + 1), :KC], back[ROWS * s : ROWS * (s + 1), KC:]], axis=0
            )
            for s in range(POINTS)
        ],
        axis=1,
    )
    spectra = dot_tn(turn, back)
    adjoint_real = jnp.zeros((KR, KC), jnp.float32)
    adjoint_imag = jnp.zeros((KR, KC), jnp.float32)
    for s in range(POINTS):
        now = spectra[:, KC * s : KC * (s + 1)]
        adjoint_real = adjoint_real + opened[s] * now[:KR]
        adjoint_imag = adjoint_imag + opened[s] * now[KR:]
    folded = dot(jnp.concatenate([adjoint_real, adjoint_imag], axis=0), fold_columns)
    real, imag = folded[:KR], folded[KR:]
    even = lanes((KR, 2 * KC)) <= HALF
    kinds = jnp.concatenate([jnp.where(even, real, imag), jnp.where(even, -imag, real)], axis=0)
    packed = dot(fold_rows, kinds)
    last = dot_nt(pick, packed[:, KC:])
    return jnp.concatenate([packed[:KR, :KC], packed[KR : KR + 8, :KC] + last], axis=0)


def final_math(total, mask, rows, turn_cos, turn_sin, columns, last_column):
    part = dot(rows[:, :40], total)
    edge = jnp.sum(rows * total[KR + 1 : KR + 2], axis=1, keepdims=True)
    turned = part * turn_cos + roll(part, HALF) * turn_sin
    grad = dot(turned, columns) + edge * last_column
    opening = logistic(mask)
    return grad * opening * (1.0 - opening)


VMEM = pl.BlockSpec(memory_space=pltpu.VMEM)
SMEM = pl.BlockSpec(memory_space=pltpu.SMEM)


def call(body, shape, name, scalars, arrays):
    return pl.pallas_call(
        body,
        in_specs=[SMEM] * len(scalars) + [VMEM] * len(arrays),
        out_specs=VMEM,
        out_shape=jax.ShapeDtypeStruct(shape, jnp.float32),
        name=name,
    )(*scalars, *arrays)


def pick_block(table, index):
    return lax.dynamic_index_in_dim(jnp.asarray(table), index, 0, False)


def columns_part(mask_param):
    tables = (column_table(), *turn_tables())
    if not KERNELS:
        message = columns_math(mask_param, *tables)
        return jnp.broadcast_to(message[None], (ROW_BLOCKS, *message.shape))

    def kernel(mask_ref, base_ref, cos_ref, sin_ref, out_ref):
        message = columns_math(mask_ref[...], base_ref[...], cos_ref[...], sin_ref[...])
        for b in range(ROW_BLOCKS):
            out_ref[b] = message

    return call(kernel, (ROW_BLOCKS, 24, KC), "columns_part", (), (mask_param, *tables))


def middle_part(half, row_index, weight, row_shift, col_shift, heard, target):
    target = target.reshape(NEAR * ROWS, SHARE)
    arrays = (
        heard,
        target,
        pick_block(own_row_table(), row_index),
        *band_tables(),
        spread_table(),
        f32(sample_table()),
        f32(interpolation_table()),
        *fold_tables(),
    )
    scalars = (half.reshape(1), weight, row_shift, col_shift)
    if not KERNELS:
        message = middle_math(half, *scalars[1:], *arrays)
        return jnp.broadcast_to(message[None], (8, *message.shape))

    def kernel(half_ref, weight_ref, row_ref, col_ref, heard_ref, *refs):
        *refs, out_ref = refs
        message = middle_math(
            half_ref[0], weight_ref, row_ref, col_ref, heard_ref, *[ref[...] for ref in refs]
        )
        for b in range(8):
            out_ref[b] = message

    return call(kernel, (8, 40, KC), "middle_part", scalars, arrays)


def repeat_sum(received):
    if not KERNELS:
        return jnp.broadcast_to(jnp.sum(received, axis=0)[None], received.shape)

    def kernel(in_ref, out_ref):
        total = in_ref[0]
        for b in range(1, received.shape[0]):
            total = total + in_ref[b]
        for b in range(received.shape[0]):
            out_ref[b] = total

    return call(kernel, received.shape, "repeat_sum", (), (received,))


def final_part(src_index, row_index, received, mask_param):
    rows, columns, last_column = final_tables()
    arrays = (
        received,
        lax.dynamic_slice_in_dim(mask_param, src_index * SHARE, SHARE, 1),
        pick_block(rows, row_index),
        *[pick_block(table.reshape(BLOCKS, 1, KC), src_index) for table in turn_tables()],
        columns,
        last_column,
    )
    if not KERNELS:
        return final_math(jnp.sum(received, axis=0), *arrays[1:])

    def kernel(in_ref, *refs):
        *refs, out_ref = refs
        total = in_ref[0]
        for b in range(1, received.shape[0]):
            total = total + in_ref[b]
        out_ref[...] = final_math(total, *[ref[...] for ref in refs])

    return call(kernel, (ROWS, SHARE), "final_part", (), arrays)


def swap(values, axis):
    return lax.all_to_all(values, axis, 0, 0, tiled=True)


def local(mask_param, target, source_weight, row_shift, col_shift):
    half = lax.axis_index("zh")
    src_index = lax.axis_index(("zh", "x", "c"))
    row_index = lax.axis_index(("zl", "y"))
    near = swap(jnp.broadcast_to(target[None], (NEAR, *target.shape)), ("x", "c"))
    heard = swap(columns_part(mask_param), ("zl", "y"))
    message = middle_part(half, row_index, source_weight, row_shift, col_shift, heard, near)
    message = repeat_sum(swap(message, "y"))
    return final_part(src_index, row_index, swap(message, ("zh", "zl")), mask_param)


def solution(mesh):
    fine = Mesh(mesh.devices.reshape(2, 4, 2, 4, 8), ("zh", "x", "c", "zl", "y"))
    rows, src = ("zl", "y"), ("zh", "x", "c")
    placed = (P(rows, None), P(rows, src), P(), P(), P())
    return jax.shard_map(
        local, mesh=fine, in_specs=placed, out_specs=P(rows, src), check_vma=False
    )
```

```python
import math

import jax
import jax.numpy as jnp
import numpy as np
from jax import lax
from jax.experimental import pallas as pl
from jax.experimental.pallas import tpu as pltpu
from jax.sharding import Mesh
from jax.sharding import PartitionSpec as P

steepness = 250.0
threshold_level = 0.25
loss_weight = 8.0
highest = lax.Precision.HIGHEST
KERNELS = True

NR = 512
NC = 8192
KR = 32
KC = 128
MC = 256
HALF = KC // 2
SHARE = 512
BLOCKS = NC // SHARE
ROWS = 16
ROW_BLOCKS = NR // ROWS
POINTS = 16
NEAR = 8
STEP = MC // BLOCKS
UNIT = 1.0 / math.sqrt(NR * NC)


def f32(table):
    return np.ascontiguousarray(np.asarray(table, dtype=np.float32))


def wave(frequency, position, period):
    angle = (np.outer(frequency, position) % period) * (2.0 * np.pi / period)
    return np.cos(angle), np.sin(angle)


def column_table():
    cos, sin = wave(np.arange(HALF + 1), np.arange(SHARE), NC)
    table = np.zeros((2 * KC, SHARE))
    table[:HALF] = cos[:HALF]
    table[HALF] = cos[HALF]
    table[HALF + 1 : KC] = -sin[1:HALF]
    table[KC] = -sin[HALF]
    return f32(table.T)


def turn_tables():
    cos, sin = wave(np.arange(BLOCKS), np.arange(HALF), BLOCKS)
    return f32(np.concatenate([cos, cos], axis=1)), f32(np.concatenate([sin, -sin], axis=1))


def spread_table():
    table = np.zeros((KC, 2 * KC))
    for frequency in range(-HALF, HALF):
        size, at = abs(frequency), frequency + HALF
        table[size, at] = 1.0
        if 0 < size < HALF:
            table[HALF + size, KC + at] = 1.0 if frequency > 0 else -1.0
    return f32(table)


def band_tables():
    cos, sin = wave(np.arange(KR) - KR // 2, np.arange(NR), NR)
    rows = np.concatenate([cos, sin]) * (UNIT * UNIT)
    split = rows.reshape(2 * KR, ROW_BLOCKS, 2, ROWS // 2)
    edge = np.concatenate([split[:, :, 0].reshape(2 * KR, -1), split[:, :, 1].reshape(2 * KR, -1)])
    return f32(rows), f32(edge)


def own_row_table():
    cos, sin = wave(np.arange(NR), np.arange(KR) - KR // 2, NR)
    cos = cos.reshape(ROW_BLOCKS, ROWS, KR)
    sin = sin.reshape(ROW_BLOCKS, ROWS, KR)
    turn = np.concatenate(
        [np.concatenate([cos, -sin], axis=2), np.concatenate([sin, cos], axis=2)], axis=1
    )
    return f32(turn)


def sample_table():
    cos, sin = wave(np.arange(KC) - HALF, np.arange(MC), MC)
    return np.block([[cos, sin], [-sin, cos]])


def interpolation_table():
    place = (np.arange(MC)[:, None] * (NC // MC) - np.arange(SHARE)[None, :]) % NC
    total = np.ones_like(place, dtype=np.float64)
    for k in range(1, HALF + 1):
        total += 2.0 * np.cos(((place * k) % NC) * (2.0 * np.pi / NC))
    return total / MC


def fold_tables():
    columns = np.zeros((KC, 2 * KC))
    for frequency in range(-HALF, HALF):
        at, size = frequency + HALF, abs(frequency)
        columns[at, size] = 1.0
        if size > 0:
            columns[at, HALF + size] = -1.0 if frequency > 0 else 1.0
    columns[0, KC] = 1.0
    columns[0, HALF] = 1.0
    rows = np.zeros((KC, 2 * KR))
    for frequency in range(-KR // 2, KR // 2):
        at, size = frequency + KR // 2, abs(frequency)
        rows[size, at] = 1.0
        if size > 0:
            rows[KR // 2 + size, KR + at] = float(np.sign(frequency))
    pick = np.zeros((8, KC))
    pick[1, 0] = 1.0
    return f32(columns), f32(rows), f32(pick)


def final_tables():
    cos, sin = wave(np.arange(NR), np.arange(KR // 2 + 1), NR)
    rows = np.zeros((NR, KC))
    rows[:, : KR // 2 + 1] = cos * UNIT
    rows[:, KR // 2 + 1 : KR + 1] = sin[:, 1:] * UNIT
    cos_y, sin_y = wave(np.arange(HALF + 1), np.arange(SHARE), NC)
    columns = np.concatenate([cos_y, sin_y[1:HALF]])
    return f32(rows.reshape(ROW_BLOCKS, ROWS, KC)), f32(columns), f32(sin_y[HALF:])


def dot(left, right):
    return jnp.dot(left, right, precision=highest, preferred_element_type=jnp.float32)


def dot_nt(left, right, precision=highest):
    return lax.dot_general(
        left, right, (((1,), (1,)), ((), ())), precision=precision, preferred_element_type=jnp.float32
    )


def split(values):
    high = values.astype(jnp.bfloat16)
    return high, (values - high.astype(jnp.float32)).astype(jnp.bfloat16)


def dot3_nt(left, right):
    high, low = split(left)
    right_high, right_low = split(right)
    one = lambda a, b: dot_nt(a, b, None)
    return one(high, right_high) + (one(high, right_low) + one(low, right_high))


def dot_tn(left, right):
    return lax.dot_general(
        left, right, (((0,), (0,)), ((), ())), precision=highest, preferred_element_type=jnp.float32
    )


def logistic(values):
    return 1.0 / (1.0 + jnp.exp(-values))


def roll(values, shift):
    if KERNELS:
        return pltpu.roll(values, shift, axis=1)
    return jnp.roll(values, shift, axis=1)


def lanes(shape):
    return lax.broadcasted_iota(jnp.int32, shape, 1)


def columns_math(mask, base, turn_cos, turn_sin):
    stacked = jnp.concatenate(
        [logistic(mask[:, SHARE * b : SHARE * (b + 1)]) for b in range(BLOCKS)], axis=0
    )
    parts = dot(stacked, base)
    main = jnp.zeros((ROWS, KC), jnp.float32)
    edge = jnp.zeros((ROWS, KC), jnp.float32)
    for b in range(BLOCKS):
        part = parts[ROWS * b : ROWS * (b + 1)]
        first = part[:, :KC]
        main = main + first * turn_cos[b : b + 1] + roll(first, HALF) * turn_sin[b : b + 1]
        edge = edge + part[:, KC:]
    return jnp.concatenate([main, edge[:8] + roll(edge[8:], 1)], axis=0)


def pupil(row_shift, col_shift):
    radius_rows = KR // 4
    radius_cols = KC // 4
    fr = lax.broadcasted_iota(jnp.int32, (KR, KC), 0) - KR // 2 + row_shift
    fc = lanes((KR, KC)) - HALF + col_shift
    limit_value = (radius_rows * radius_cols) ** 2
    inside = fr * fr * (radius_cols * radius_cols) + fc * fc * (radius_rows * radius_rows)
    return (inside <= limit_value).astype(jnp.float32)


def middle_math(
    half,
    weight,
    row_shift,
    col_shift,
    heard,
    target,
    turn,
    rows,
    rows_edge,
    spread,
    to_samples,
    interpolate,
    fold_columns,
    fold_rows,
    pick,
):
    main = jnp.concatenate([heard[b, :ROWS] for b in range(ROW_BLOCKS)], axis=0)
    edge = jnp.concatenate([heard[b, ROWS:] for b in range(ROW_BLOCKS)], axis=0)
    both = dot(dot(rows, main), spread)
    edges = dot(rows_edge, edge)
    edge_column = edges[: 2 * KR, 0:1] + edges[2 * KR :, 1:2]
    real = both[:, :KC]
    imag = both[:, KC:] - jnp.where(lanes((2 * KR, KC)) == 0, edge_column, 0.0)
    band_real = real[:KR] + imag[KR:]
    band_imag = imag[:KR] - real[KR:]

    opened = [pupil(row_shift[s], col_shift[s]) for s in range(POINTS)]
    masked = jnp.concatenate(
        [
            jnp.concatenate([band_real * opened[s], band_imag * opened[s]], axis=0)
            for s in range(POINTS)
        ],
        axis=1,
    )
    head = dot(turn, masked)
    head = jnp.concatenate(
        [
            jnp.concatenate(
                [head[:ROWS, KC * s : KC * (s + 1)], head[ROWS:, KC * s : KC * (s + 1)]], axis=1
            )
            for s in range(POINTS)
        ],
        axis=0,
    )
    field = dot(head, to_samples)
    samples = jnp.zeros((ROWS, MC), jnp.float32)
    total = 0.0
    for s in range(POINTS):
        now = field[ROWS * s : ROWS * (s + 1)]
        samples = samples + weight[s] * (now[:, :MC] * now[:, :MC] + now[:, MC:] * now[:, MC:])
        total = total + weight[s]
    share = 1.0 / jnp.full((ROWS, MC), total, jnp.float32)
    samples = samples * share
    samples = jnp.where(half == 1, roll(samples, MC // 2), samples)
    near = jnp.concatenate([samples] + [roll(samples, MC - STEP * j) for j in range(1, NEAR)], axis=0)
    intensity = dot(near, interpolate)
    resist = logistic(steepness * (intensity - threshold_level))
    slope = (
        2.0
        * loss_weight
        * (resist - target.astype(jnp.float32))
        * steepness
        * resist
        * (1.0 - resist)
    )
    lows = dot3_nt(slope, interpolate)
    low = lows[:ROWS]
    for j in range(1, NEAR):
        low = low + roll(lows[ROWS * j : ROWS * (j + 1)], STEP * j)
    low = jnp.where(half == 1, roll(low, MC // 2), low)
    low = low * share * (2.0 * UNIT)
    wide = jnp.concatenate([low, low], axis=1)
    scaled = jnp.concatenate(
        [(weight[s] * wide) * field[ROWS * s : ROWS * (s + 1)] for s in range(POINTS)], axis=0
    )
    back = dot3_nt(scaled, to_samples)
    back = jnp.concatenate(
        [
            jnp.concatenate(
                [back[ROWS * s : ROWS * (s + 1), :KC], back[ROWS * s : ROWS * (s + 1), KC:]], axis=0
            )
            for s in range(POINTS)
        ],
        axis=1,
    )
    spectra = dot_tn(turn, back)
    adjoint_real = jnp.zeros((KR, KC), jnp.float32)
    adjoint_imag = jnp.zeros((KR, KC), jnp.float32)
    for s in range(POINTS):
        now = spectra[:, KC * s : KC * (s + 1)]
        adjoint_real = adjoint_real + opened[s] * now[:KR]
        adjoint_imag = adjoint_imag + opened[s] * now[KR:]
    folded = dot(jnp.concatenate([adjoint_real, adjoint_imag], axis=0), fold_columns)
    real, imag = folded[:KR], folded[KR:]
    even = lanes((KR, 2 * KC)) <= HALF
    kinds = jnp.concatenate([jnp.where(even, real, imag), jnp.where(even, -imag, real)], axis=0)
    packed = dot(fold_rows, kinds)
    last = dot_nt(pick, packed[:, KC:])
    return jnp.concatenate([packed[:KR, :KC], packed[KR : KR + 8, :KC] + last], axis=0)


def final_math(total, mask, rows, turn_cos, turn_sin, columns, last_column):
    part = dot(rows[:, :40], total)
    edge = jnp.sum(rows * total[KR + 1 : KR + 2], axis=1, keepdims=True)
    turned = part * turn_cos + roll(part, HALF) * turn_sin
    grad = dot(turned, columns) + edge * last_column
    opening = logistic(mask)
    return grad * opening * (1.0 - opening)


VMEM = pl.BlockSpec(memory_space=pltpu.VMEM)
SMEM = pl.BlockSpec(memory_space=pltpu.SMEM)


def call(body, shape, name, scalars, arrays):
    arrays = [pltpu.with_memory_space_constraint(array, pltpu.VMEM) for array in arrays]
    return pl.pallas_call(
        body,
        in_specs=[SMEM] * len(scalars) + [VMEM] * len(arrays),
        out_specs=VMEM,
        out_shape=jax.ShapeDtypeStruct(shape, jnp.float32),
        name=name,
    )(*scalars, *arrays)


def pick_block(table, index):
    return lax.dynamic_index_in_dim(jnp.asarray(table), index, 0, False)


def columns_part(mask_param):
    tables = (column_table(), *turn_tables())
    if not KERNELS:
        message = columns_math(mask_param, *tables)
        return jnp.broadcast_to(message[None], (ROW_BLOCKS, *message.shape))

    def kernel(mask_ref, base_ref, cos_ref, sin_ref, out_ref):
        message = columns_math(mask_ref[...], base_ref[...], cos_ref[...], sin_ref[...])
        for b in range(ROW_BLOCKS):
            out_ref[b] = message

    return call(kernel, (ROW_BLOCKS, 24, KC), "columns_part", (), (mask_param, *tables))


def middle_part(half, row_index, weight, row_shift, col_shift, heard, target):
    target = target.reshape(NEAR * ROWS, SHARE)
    arrays = (
        heard,
        target,
        pick_block(own_row_table(), row_index),
        *band_tables(),
        spread_table(),
        f32(sample_table()),
        f32(interpolation_table()),
        *fold_tables(),
    )
    scalars = (half.reshape(1), weight, row_shift, col_shift)
    if not KERNELS:
        message = middle_math(half, *scalars[1:], *arrays)
        return jnp.broadcast_to(message[None], (8, *message.shape))

    def kernel(half_ref, weight_ref, row_ref, col_ref, heard_ref, *refs):
        *refs, out_ref = refs
        message = middle_math(
            half_ref[0], weight_ref, row_ref, col_ref, heard_ref, *[ref[...] for ref in refs]
        )
        for b in range(8):
            out_ref[b] = message

    return call(kernel, (8, 40, KC), "middle_part", scalars, arrays)


def repeat_sum(received):
    if not KERNELS:
        return jnp.broadcast_to(jnp.sum(received, axis=0)[None], received.shape)

    def kernel(in_ref, out_ref):
        total = in_ref[0]
        for b in range(1, received.shape[0]):
            total = total + in_ref[b]
        for b in range(received.shape[0]):
            out_ref[b] = total

    return call(kernel, received.shape, "repeat_sum", (), (received,))


def final_part(src_index, row_index, received, mask_param):
    rows, columns, last_column = final_tables()
    arrays = (
        received,
        lax.dynamic_slice_in_dim(mask_param, src_index * SHARE, SHARE, 1),
        pick_block(rows, row_index),
        *[pick_block(table.reshape(BLOCKS, 1, KC), src_index) for table in turn_tables()],
        columns,
        last_column,
    )
    if not KERNELS:
        return final_math(jnp.sum(received, axis=0), *arrays[1:])

    def kernel(in_ref, *refs):
        *refs, out_ref = refs
        total = in_ref[0]
        for b in range(1, received.shape[0]):
            total = total + in_ref[b]
        out_ref[...] = final_math(total, *[ref[...] for ref in refs])

    return call(kernel, (ROWS, SHARE), "final_part", (), arrays)


def swap(values, axis):
    return lax.all_to_all(values, axis, 0, 0, tiled=True)


def local(mask_param, target, source_weight, row_shift, col_shift):
    half = lax.axis_index("zh")
    src_index = lax.axis_index(("zh", "x", "c"))
    row_index = lax.axis_index(("zl", "y"))
    near = swap(jnp.broadcast_to(target[None], (NEAR, *target.shape)), ("x", "c"))
    heard = swap(columns_part(mask_param), ("zl", "y"))
    message = middle_part(half, row_index, source_weight, row_shift, col_shift, heard, near)
    message = repeat_sum(swap(message, "y"))
    return final_part(src_index, row_index, swap(message, ("zh", "zl")), mask_param)


def solution(mesh):
    fine = Mesh(mesh.devices.reshape(2, 4, 2, 4, 8), ("zh", "x", "c", "zl", "y"))
    rows, src = ("zl", "y"), ("zh", "x", "c")
    placed = (P(rows, None), P(rows, src), P(), P(), P())
    return jax.shard_map(
        local, mesh=fine, in_specs=placed, out_specs=P(rows, src), check_vma=False
    )
```

```python
import math

import jax
import jax.numpy as jnp
import numpy as np
from jax import lax
from jax.experimental import pallas as pl
from jax.experimental.pallas import tpu as pltpu
from jax.sharding import Mesh
from jax.sharding import PartitionSpec as P

steepness = 250.0
threshold_level = 0.25
loss_weight = 8.0
highest = lax.Precision.HIGHEST
KERNELS = True

NR = 512
NC = 8192
KR = 32
KC = 128
MC = 256
HALF = KC // 2
SHARE = 512
BLOCKS = NC // SHARE
ROWS = 16
ROW_BLOCKS = NR // ROWS
POINTS = 16
NEAR = 8
STEP = MC // BLOCKS
LINES = ROWS + 1
UNIT = 1.0 / math.sqrt(NR * NC)


def f32(table):
    return np.ascontiguousarray(np.asarray(table, dtype=np.float32))


def wave(frequency, position, period):
    angle = (np.outer(frequency, position) % period) * (2.0 * np.pi / period)
    return np.cos(angle), np.sin(angle)


def column_table():
    cos, sin = wave(np.arange(HALF + 1), np.arange(SHARE), NC)
    table = np.zeros((2 * KC, SHARE))
    table[:HALF] = cos[:HALF]
    table[HALF] = cos[HALF]
    table[HALF + 1 : KC] = -sin[1:HALF]
    table[KC] = -sin[HALF]
    return f32(table[: KC + 8])


def turn_tables():
    cos, sin = wave(np.arange(BLOCKS), np.arange(HALF), BLOCKS)
    return f32(np.concatenate([cos, cos], axis=1)), f32(np.concatenate([sin, -sin], axis=1))


def spread_table():
    table = np.zeros((KC, 2 * KC))
    for frequency in range(-HALF, HALF):
        size, at = abs(frequency), frequency + HALF
        table[size, at] = 1.0
        if 0 < size < HALF:
            table[HALF + size, KC + at] = 1.0 if frequency > 0 else -1.0
    return f32(table)


def band_tables():
    frequency = np.arange(KR) - KR // 2
    rows = np.concatenate(wave(frequency, np.arange(NR), NR)) * (UNIT * UNIT)
    inner = np.zeros((2 * KR, KC))
    inner[:, :ROWS] = np.concatenate(wave(frequency, np.arange(ROWS), NR)) * (UNIT * UNIT)
    outer = np.concatenate(wave(frequency, np.arange(ROW_BLOCKS) * ROWS, NR))
    return f32(rows), f32(inner), f32(outer)


def own_row_table():
    cos, sin = wave(np.arange(NR), np.arange(KR) - KR // 2, NR)
    cos = cos.reshape(ROW_BLOCKS, ROWS, KR)
    sin = sin.reshape(ROW_BLOCKS, ROWS, KR)
    turn = np.concatenate(
        [np.concatenate([cos, -sin], axis=2), np.concatenate([sin, cos], axis=2)], axis=1
    )
    return f32(turn)


def sample_table():
    cos, sin = wave(np.arange(KC) - HALF, np.arange(MC), MC)
    return np.block([[cos, sin], [-sin, cos]])


def interpolation_table():
    place = (np.arange(MC)[:, None] * (NC // MC) - np.arange(SHARE)[None, :]) % NC
    total = np.ones_like(place, dtype=np.float64)
    for k in range(1, HALF + 1):
        total += 2.0 * np.cos(((place * k) % NC) * (2.0 * np.pi / NC))
    return total / MC


def fold_tables():
    columns = np.zeros((KC, 2 * KC))
    for frequency in range(-HALF, HALF):
        at, size = frequency + HALF, abs(frequency)
        columns[at, size] = 1.0
        if size > 0:
            columns[at, HALF + size] = -1.0 if frequency > 0 else 1.0
    columns[0, KC] = 1.0
    columns[0, HALF] = 1.0
    rows = np.zeros((KC, 2 * KR))
    for frequency in range(-KR // 2, KR // 2):
        at, size = frequency + KR // 2, abs(frequency)
        rows[size, at] = 1.0
        if size > 0:
            rows[KR // 2 + size, KR + at] = float(np.sign(frequency))
    pick = np.zeros((8, KC))
    pick[1, 0] = 1.0
    return f32(columns), f32(rows), f32(pick)


def final_tables():
    cos, sin = wave(np.arange(NR), np.arange(KR // 2 + 1), NR)
    rows = np.zeros((NR, KC))
    rows[:, : KR // 2 + 1] = cos * UNIT
    rows[:, KR // 2 + 1 : KR + 1] = sin[:, 1:] * UNIT
    cos_y, sin_y = wave(np.arange(HALF + 1), np.arange(SHARE), NC)
    columns = np.concatenate([cos_y, sin_y[1:HALF]])
    return f32(rows.reshape(ROW_BLOCKS, ROWS, KC)), f32(columns), f32(sin_y[HALF:])


def dot(left, right):
    return jnp.dot(left, right, precision=highest, preferred_element_type=jnp.float32)


def dot_nt(left, right, precision=highest):
    return lax.dot_general(
        left, right, (((1,), (1,)), ((), ())), precision=precision, preferred_element_type=jnp.float32
    )


def split(values):
    high = values.astype(jnp.bfloat16)
    return high, (values - high.astype(jnp.float32)).astype(jnp.bfloat16)


def dot3_nt(left, right):
    high, low = split(left)
    right_high, right_low = split(right)
    one = lambda a, b: dot_nt(a, b, None)
    return one(high, right_high) + (one(high, right_low) + one(low, right_high))


def dot_tn(left, right):
    return lax.dot_general(
        left, right, (((0,), (0,)), ((), ())), precision=highest, preferred_element_type=jnp.float32
    )


def logistic(values):
    return 1.0 / (1.0 + jnp.exp(-values))


def roll(values, shift):
    if KERNELS:
        return pltpu.roll(values, shift, axis=1)
    return jnp.roll(values, shift, axis=1)


def lanes(shape):
    return lax.broadcasted_iota(jnp.int32, shape, 1)


def columns_math(mask, base, turn_cos, turn_sin, pick):
    stacked = jnp.concatenate(
        [logistic(mask[:, SHARE * b : SHARE * (b + 1)]) for b in range(BLOCKS)], axis=0
    )
    parts = dot_nt(stacked, base)
    main = jnp.zeros((ROWS, KC), jnp.float32)
    edge = jnp.zeros((ROWS, 8), jnp.float32)
    for b in range(BLOCKS):
        part = parts[ROWS * b : ROWS * (b + 1)]
        first = part[:, :KC]
        main = main + first * turn_cos[b : b + 1] + roll(first, HALF) * turn_sin[b : b + 1]
        edge = edge + part[:, KC:]
    edge = jnp.concatenate([edge, jnp.zeros((KC - ROWS, 8), jnp.float32)], axis=0)
    return main, dot_nt(pick[:, :8], edge)[1:2]


def pupil(row_shift, col_shift):
    radius_rows = KR // 4
    radius_cols = KC // 4
    fr = lax.broadcasted_iota(jnp.int32, (KR, KC), 0) - KR // 2 + row_shift
    fc = lanes((KR, KC)) - HALF + col_shift
    limit_value = (radius_rows * radius_cols) ** 2
    inside = fr * fr * (radius_cols * radius_cols) + fc * fc * (radius_rows * radius_rows)
    return (inside <= limit_value).astype(jnp.float32)


def middle_math(
    half,
    weight,
    row_shift,
    col_shift,
    main,
    edge,
    target,
    turn,
    rows,
    inner,
    outer,
    spread,
    to_samples,
    interpolate,
    fold_columns,
    fold_rows,
    pick,
):
    both = dot(dot(rows, main), spread)
    inside = dot_nt(inner, edge)
    in_cos, in_sin = inside[:KR], inside[KR:]
    out_cos, out_sin = outer[:KR], outer[KR:]
    edge_cos = jnp.sum(out_cos * in_cos - out_sin * in_sin, axis=1, keepdims=True)
    edge_sin = jnp.sum(out_sin * in_cos + out_cos * in_sin, axis=1, keepdims=True)
    edge_column = jnp.concatenate([edge_cos, edge_sin], axis=0)
    real = both[:, :KC]
    imag = both[:, KC:] - jnp.where(lanes((2 * KR, KC)) == 0, edge_column, 0.0)
    band_real = real[:KR] + imag[KR:]
    band_imag = imag[:KR] - real[KR:]

    opened = [pupil(row_shift[s], col_shift[s]) for s in range(POINTS)]
    masked = jnp.concatenate(
        [
            jnp.concatenate([band_real * opened[s], band_imag * opened[s]], axis=0)
            for s in range(POINTS)
        ],
        axis=1,
    )
    head = dot(turn, masked)
    head = jnp.concatenate(
        [
            jnp.concatenate(
                [head[:ROWS, KC * s : KC * (s + 1)], head[ROWS:, KC * s : KC * (s + 1)]], axis=1
            )
            for s in range(POINTS)
        ],
        axis=0,
    )
    field = dot(head, to_samples)
    samples = jnp.zeros((ROWS, MC), jnp.float32)
    total = 0.0
    for s in range(POINTS):
        now = field[ROWS * s : ROWS * (s + 1)]
        samples = samples + weight[s] * (now[:, :MC] * now[:, :MC] + now[:, MC:] * now[:, MC:])
        total = total + weight[s]
    share = 1.0 / jnp.full((ROWS, MC), total, jnp.float32)
    samples = samples * share
    samples = jnp.where(half == 1, roll(samples, MC // 2), samples)
    near = jnp.concatenate([samples] + [roll(samples, MC - STEP * j) for j in range(1, NEAR)], axis=0)
    intensity = dot(near, interpolate)
    resist = logistic(steepness * (intensity - threshold_level))
    slope = (
        2.0
        * loss_weight
        * (resist - target.astype(jnp.float32))
        * steepness
        * resist
        * (1.0 - resist)
    )
    lows = dot3_nt(slope, interpolate)
    low = lows[:ROWS]
    for j in range(1, NEAR):
        low = low + roll(lows[ROWS * j : ROWS * (j + 1)], STEP * j)
    low = jnp.where(half == 1, roll(low, MC // 2), low)
    low = low * share * (2.0 * UNIT)
    wide = jnp.concatenate([low, low], axis=1)
    scaled = jnp.concatenate(
        [(weight[s] * wide) * field[ROWS * s : ROWS * (s + 1)] for s in range(POINTS)], axis=0
    )
    back = dot3_nt(scaled, to_samples)
    back = jnp.concatenate(
        [
            jnp.concatenate(
                [back[ROWS * s : ROWS * (s + 1), :KC], back[ROWS * s : ROWS * (s + 1), KC:]], axis=0
            )
            for s in range(POINTS)
        ],
        axis=1,
    )
    spectra = dot_tn(turn, back)
    adjoint_real = jnp.zeros((KR, KC), jnp.float32)
    adjoint_imag = jnp.zeros((KR, KC), jnp.float32)
    for s in range(POINTS):
        now = spectra[:, KC * s : KC * (s + 1)]
        adjoint_real = adjoint_real + opened[s] * now[:KR]
        adjoint_imag = adjoint_imag + opened[s] * now[KR:]
    folded = dot(jnp.concatenate([adjoint_real, adjoint_imag], axis=0), fold_columns)
    real, imag = folded[:KR], folded[KR:]
    even = lanes((KR, 2 * KC)) <= HALF
    kinds = jnp.concatenate([jnp.where(even, real, imag), jnp.where(even, -imag, real)], axis=0)
    packed = dot(fold_rows, kinds)
    last = dot_nt(pick, packed[:, KC:])
    return jnp.concatenate([packed[:KR, :KC], packed[KR : KR + 8, :KC] + last], axis=0)


def final_math(total, mask, rows, turn_cos, turn_sin, columns, last_column):
    part = dot(rows[:, :40], total)
    edge = jnp.sum(rows * total[KR + 1 : KR + 2], axis=1, keepdims=True)
    turned = part * turn_cos + roll(part, HALF) * turn_sin
    grad = dot(turned, columns) + edge * last_column
    opening = logistic(mask)
    return grad * opening * (1.0 - opening)


VMEM = pl.BlockSpec(memory_space=pltpu.VMEM)
SMEM = pl.BlockSpec(memory_space=pltpu.SMEM)


def call(body, outputs, name, scalars, arrays):
    arrays = [pltpu.with_memory_space_constraint(array, pltpu.VMEM) for array in arrays]
    return pl.pallas_call(
        body,
        in_specs=[SMEM] * len(scalars) + [VMEM] * len(arrays),
        out_specs=jax.tree.map(lambda _: VMEM, outputs),
        out_shape=outputs,
        name=name,
    )(*scalars, *arrays)


def plain(*shape):
    return jax.ShapeDtypeStruct(shape, jnp.float32)


def pick_block(table, index):
    return lax.dynamic_index_in_dim(jnp.asarray(table), index, 0, False)


def columns_part(mask_param):
    tables = (column_table(), *turn_tables(), fold_tables()[2])
    if not KERNELS:
        return repeated(jnp.concatenate(columns_math(mask_param, *tables)), ROW_BLOCKS)

    def kernel(mask_ref, *refs):
        *refs, out_ref = refs
        main, edge = columns_math(mask_ref[...], *[ref[...] for ref in refs])
        for b in range(ROW_BLOCKS):
            out_ref[LINES * b : LINES * b + ROWS] = main
            out_ref[LINES * b + ROWS : LINES * (b + 1)] = edge

    sent = call(kernel, plain(ROW_BLOCKS * LINES, KC), "columns_part", (), (mask_param, *tables))
    return sent.reshape(ROW_BLOCKS, 1, LINES * KC)


def repeated(values, count):
    return jnp.broadcast_to(values[None], (count, *values.shape))


def middle_part(half, weight, row_shift, col_shift, heard, target, turn):
    heard = heard.reshape(ROW_BLOCKS * LINES, KC)
    arrays = (
        heard,
        target.reshape(NEAR * ROWS, SHARE),
        turn,
        *band_tables(),
        spread_table(),
        f32(sample_table()),
        f32(interpolation_table()),
        *fold_tables(),
    )
    scalars = (half.reshape(1), weight, row_shift, col_shift)
    if not KERNELS:
        lines = heard.reshape(ROW_BLOCKS, LINES, KC)
        main, edge = lines[:, :ROWS].reshape(NR, KC), lines[:, ROWS]
        return repeated(middle_math(half, *scalars[1:], main, edge, *arrays[1:]), 8)

    def kernel(half_ref, weight_ref, row_ref, col_ref, heard_ref, *refs):
        *refs, out_ref = refs
        main = jnp.concatenate(
            [heard_ref[LINES * b : LINES * b + ROWS] for b in range(ROW_BLOCKS)], axis=0
        )
        edge = heard_ref[pl.ds(ROWS, ROW_BLOCKS, stride=LINES)]
        message = middle_math(
            half_ref[0], weight_ref, row_ref, col_ref, main, edge, *[ref[...] for ref in refs]
        )
        for b in range(8):
            out_ref[b] = message

    return call(kernel, plain(8, 40, KC), "middle_part", scalars, arrays)


def repeat_sum(received):
    if not KERNELS:
        return jnp.broadcast_to(jnp.sum(received, axis=0)[None], received.shape)

    def kernel(in_ref, out_ref):
        total = in_ref[0]
        for b in range(1, received.shape[0]):
            total = total + in_ref[b]
        for b in range(received.shape[0]):
            out_ref[b] = total

    return call(kernel, plain(*received.shape), "repeat_sum", (), (received,))


def final_part(src_index, row_index, received, mask_param):
    rows, columns, last_column = final_tables()
    arrays = (
        received,
        lax.dynamic_slice_in_dim(mask_param, src_index * SHARE, SHARE, 1),
        pick_block(rows, row_index),
        *[pick_block(table.reshape(BLOCKS, 1, KC), src_index) for table in turn_tables()],
        columns,
        last_column,
    )
    if not KERNELS:
        return final_math(jnp.sum(received, axis=0), *arrays[1:])

    def kernel(in_ref, *refs):
        *refs, out_ref = refs
        total = in_ref[0]
        for b in range(1, received.shape[0]):
            total = total + in_ref[b]
        out_ref[...] = final_math(total, *[ref[...] for ref in refs])

    return call(kernel, plain(ROWS, SHARE), "final_part", (), arrays)


def swap(values, axis):
    return lax.all_to_all(values, axis, 0, 0, tiled=True)


def local(mask_param, target, source_weight, row_shift, col_shift):
    half = lax.axis_index("zh")
    src_index = lax.axis_index(("zh", "x", "c"))
    row_index = lax.axis_index(("zl", "y"))
    source = (source_weight, row_shift, col_shift)
    turn = pick_block(own_row_table(), row_index)
    near = swap(repeated(target, NEAR), ("x", "c"))
    heard = swap(columns_part(mask_param), ("zl", "y"))
    message = repeat_sum(swap(middle_part(half, *source, heard, near, turn), "y"))
    return final_part(src_index, row_index, swap(message, ("zh", "zl")), mask_param)


def solution(mesh):
    fine = Mesh(mesh.devices.reshape(2, 4, 2, 4, 8), ("zh", "x", "c", "zl", "y"))
    rows, src = ("zl", "y"), ("zh", "x", "c")
    placed = (P(rows, None), P(rows, src), P(), P(), P())
    return jax.shard_map(
        local, mesh=fine, in_specs=placed, out_specs=P(rows, src), check_vma=False
    )
```

```python
import math

import jax
import jax.numpy as jnp
import numpy as np
from jax import lax
from jax.experimental import pallas as pl
from jax.experimental.pallas import tpu as pltpu
from jax.sharding import Mesh
from jax.sharding import PartitionSpec as P

steepness = 250.0
threshold_level = 0.25
loss_weight = 8.0
highest = lax.Precision.HIGHEST
KERNELS = True

NR = 512
NC = 8192
KR = 32
KC = 128
MC = 256
HALF = KC // 2
SHARE = 512
BLOCKS = NC // SHARE
ROWS = 16
ROW_BLOCKS = NR // ROWS
POINTS = 16
NEAR = 8
STEP = MC // BLOCKS
LINES = ROWS + 1
UNIT = 1.0 / math.sqrt(NR * NC)


def f32(table):
    return np.ascontiguousarray(np.asarray(table, dtype=np.float32))


def wave(frequency, position, period):
    angle = (np.outer(frequency, position) % period) * (2.0 * np.pi / period)
    return np.cos(angle), np.sin(angle)


def column_table():
    cos, sin = wave(np.arange(HALF + 1), np.arange(SHARE), NC)
    table = np.zeros((2 * KC, SHARE))
    table[:HALF] = cos[:HALF]
    table[HALF] = cos[HALF]
    table[HALF + 1 : KC] = -sin[1:HALF]
    table[KC] = -sin[HALF]
    return f32(table[: KC + 8])


def turn_tables():
    cos, sin = wave(np.arange(BLOCKS), np.arange(HALF), BLOCKS)
    return f32(np.concatenate([cos, cos], axis=1)), f32(np.concatenate([sin, -sin], axis=1))


def spread_table():
    table = np.zeros((KC, 2 * KC))
    for frequency in range(-HALF, HALF):
        size, at = abs(frequency), frequency + HALF
        table[size, at] = 1.0
        if 0 < size < HALF:
            table[HALF + size, KC + at] = 1.0 if frequency > 0 else -1.0
    return f32(table)


def band_tables():
    frequency = np.arange(KR) - KR // 2
    rows = np.concatenate(wave(frequency, np.arange(NR), NR)) * (UNIT * UNIT)
    inner = np.zeros((2 * KR, KC))
    inner[:, :ROWS] = np.concatenate(wave(frequency, np.arange(ROWS), NR)) * (UNIT * UNIT)
    outer = np.concatenate(wave(frequency, np.arange(ROW_BLOCKS) * ROWS, NR))
    return f32(rows), f32(inner), f32(outer)


def own_row_table():
    cos, sin = wave(np.arange(NR), np.arange(KR) - KR // 2, NR)
    cos = cos.reshape(ROW_BLOCKS, ROWS, KR)
    sin = sin.reshape(ROW_BLOCKS, ROWS, KR)
    turn = np.concatenate(
        [np.concatenate([cos, -sin], axis=2), np.concatenate([sin, cos], axis=2)], axis=1
    )
    return f32(turn)


def sample_table():
    cos, sin = wave(np.arange(KC) - HALF, np.arange(MC), MC)
    return np.block([[cos, sin], [-sin, cos]])


def interpolation_table():
    place = (np.arange(MC)[:, None] * (NC // MC) - np.arange(SHARE)[None, :]) % NC
    total = np.ones_like(place, dtype=np.float64)
    for k in range(1, HALF + 1):
        total += 2.0 * np.cos(((place * k) % NC) * (2.0 * np.pi / NC))
    return total / MC


def fold_tables():
    columns = np.zeros((KC, 2 * KC))
    for frequency in range(-HALF, HALF):
        at, size = frequency + HALF, abs(frequency)
        columns[at, size] = 1.0
        if size > 0:
            columns[at, HALF + size] = -1.0 if frequency > 0 else 1.0
    columns[0, KC] = 1.0
    columns[0, HALF] = 1.0
    rows = np.zeros((KC, 2 * KR))
    for frequency in range(-KR // 2, KR // 2):
        at, size = frequency + KR // 2, abs(frequency)
        rows[size, at] = 1.0
        if size > 0:
            rows[KR // 2 + size, KR + at] = float(np.sign(frequency))
    pick = np.zeros((8, KC))
    pick[1, 0] = 1.0
    return f32(columns), f32(rows), f32(pick)


def final_tables():
    cos, sin = wave(np.arange(NR), np.arange(KR // 2 + 1), NR)
    rows = np.zeros((NR, KC))
    rows[:, : KR // 2 + 1] = cos * UNIT
    rows[:, KR // 2 + 1 : KR + 1] = sin[:, 1:] * UNIT
    cos_y, sin_y = wave(np.arange(HALF + 1), np.arange(SHARE), NC)
    columns = np.concatenate([cos_y, sin_y[1:HALF]])
    return f32(rows.reshape(ROW_BLOCKS, ROWS, KC)), f32(columns), f32(sin_y[HALF:])


def dot(left, right):
    return jnp.dot(left, right, precision=highest, preferred_element_type=jnp.float32)


def dot_nt(left, right, precision=highest):
    return lax.dot_general(
        left, right, (((1,), (1,)), ((), ())), precision=precision, preferred_element_type=jnp.float32
    )


def split(values):
    high = values.astype(jnp.bfloat16)
    return high, (values - high.astype(jnp.float32)).astype(jnp.bfloat16)


def dot3_nt(left, right):
    high, low = split(left)
    right_high, right_low = split(right)
    one = lambda a, b: dot_nt(a, b, None)
    return one(high, right_high) + (one(high, right_low) + one(low, right_high))


def dot_tn(left, right):
    return lax.dot_general(
        left, right, (((0,), (0,)), ((), ())), precision=highest, preferred_element_type=jnp.float32
    )


def logistic(values):
    return 1.0 / (1.0 + jnp.exp(-values))


def roll(values, shift):
    if KERNELS:
        return pltpu.roll(values, shift, axis=1)
    return jnp.roll(values, shift, axis=1)


def lanes(shape):
    return lax.broadcasted_iota(jnp.int32, shape, 1)


def columns_math(mask, base, turn_cos, turn_sin, pick):
    stacked = jnp.concatenate(
        [logistic(mask[:, SHARE * b : SHARE * (b + 1)]) for b in range(BLOCKS)], axis=0
    )
    parts = dot_nt(stacked, base)
    main = jnp.zeros((ROWS, KC), jnp.float32)
    edge = jnp.zeros((ROWS, 8), jnp.float32)
    for b in range(BLOCKS):
        part = parts[ROWS * b : ROWS * (b + 1)]
        first = part[:, :KC]
        main = main + first * turn_cos[b : b + 1] + roll(first, HALF) * turn_sin[b : b + 1]
        edge = edge + part[:, KC:]
    edge = jnp.concatenate([edge, jnp.zeros((KC - ROWS, 8), jnp.float32)], axis=0)
    return main, dot_nt(pick[:, :8], edge)[1:2]


def pupil(row_shift, col_shift):
    radius_rows = KR // 4
    radius_cols = KC // 4
    fr = lax.broadcasted_iota(jnp.int32, (KR, KC), 0) - KR // 2 + row_shift
    fc = lanes((KR, KC)) - HALF + col_shift
    limit_value = (radius_rows * radius_cols) ** 2
    inside = fr * fr * (radius_cols * radius_cols) + fc * fc * (radius_rows * radius_rows)
    return (inside <= limit_value).astype(jnp.float32)


def field_math(
    half,
    weight,
    row_shift,
    col_shift,
    main,
    edge,
    turn,
    rows,
    inner,
    outer,
    spread,
    to_samples,
    interpolate,
):
    both = dot(dot(rows, main), spread)
    inside = dot_nt(inner, edge)
    in_cos, in_sin = inside[:KR], inside[KR:]
    out_cos, out_sin = outer[:KR], outer[KR:]
    edge_cos = jnp.sum(out_cos * in_cos - out_sin * in_sin, axis=1, keepdims=True)
    edge_sin = jnp.sum(out_sin * in_cos + out_cos * in_sin, axis=1, keepdims=True)
    edge_column = jnp.concatenate([edge_cos, edge_sin], axis=0)
    real = both[:, :KC]
    imag = both[:, KC:] - jnp.where(lanes((2 * KR, KC)) == 0, edge_column, 0.0)
    band_real = real[:KR] + imag[KR:]
    band_imag = imag[:KR] - real[KR:]

    opened = [pupil(row_shift[s], col_shift[s]) for s in range(POINTS)]
    masked = jnp.concatenate(
        [
            jnp.concatenate([band_real * opened[s], band_imag * opened[s]], axis=0)
            for s in range(POINTS)
        ],
        axis=1,
    )
    head = dot(turn, masked)
    head = jnp.concatenate(
        [
            jnp.concatenate(
                [head[:ROWS, KC * s : KC * (s + 1)], head[ROWS:, KC * s : KC * (s + 1)]], axis=1
            )
            for s in range(POINTS)
        ],
        axis=0,
    )
    field = dot(head, to_samples)
    samples = jnp.zeros((ROWS, MC), jnp.float32)
    total = 0.0
    for s in range(POINTS):
        now = field[ROWS * s : ROWS * (s + 1)]
        samples = samples + weight[s] * (now[:, :MC] * now[:, :MC] + now[:, MC:] * now[:, MC:])
        total = total + weight[s]
    share = 1.0 / jnp.full((ROWS, MC), total, jnp.float32)
    samples = samples * share
    samples = jnp.where(half == 1, roll(samples, MC // 2), samples)
    near = jnp.concatenate([samples] + [roll(samples, MC - STEP * j) for j in range(1, NEAR)], axis=0)
    intensity = dot(near, interpolate)
    resist = logistic(steepness * (intensity - threshold_level))
    return field, resist


def adjoint_math(
    half,
    weight,
    row_shift,
    col_shift,
    target,
    resist,
    field,
    turn,
    to_samples,
    interpolate,
    fold_columns,
    fold_rows,
    pick,
):
    opened = [pupil(row_shift[s], col_shift[s]) for s in range(POINTS)]
    total = 0.0
    for s in range(POINTS):
        total = total + weight[s]
    share = 1.0 / jnp.full((ROWS, MC), total, jnp.float32)
    slope = (
        2.0
        * loss_weight
        * (resist - target.astype(jnp.float32))
        * steepness
        * resist
        * (1.0 - resist)
    )
    lows = dot3_nt(slope, interpolate)
    low = lows[:ROWS]
    for j in range(1, NEAR):
        low = low + roll(lows[ROWS * j : ROWS * (j + 1)], STEP * j)
    low = jnp.where(half == 1, roll(low, MC // 2), low)
    low = low * share * (2.0 * UNIT)
    wide = jnp.concatenate([low, low], axis=1)
    scaled = jnp.concatenate(
        [(weight[s] * wide) * field[ROWS * s : ROWS * (s + 1)] for s in range(POINTS)], axis=0
    )
    back = dot3_nt(scaled, to_samples)
    back = jnp.concatenate(
        [
            jnp.concatenate(
                [back[ROWS * s : ROWS * (s + 1), :KC], back[ROWS * s : ROWS * (s + 1), KC:]], axis=0
            )
            for s in range(POINTS)
        ],
        axis=1,
    )
    spectra = dot_tn(turn, back)
    adjoint_real = jnp.zeros((KR, KC), jnp.float32)
    adjoint_imag = jnp.zeros((KR, KC), jnp.float32)
    for s in range(POINTS):
        now = spectra[:, KC * s : KC * (s + 1)]
        adjoint_real = adjoint_real + opened[s] * now[:KR]
        adjoint_imag = adjoint_imag + opened[s] * now[KR:]
    folded = dot(jnp.concatenate([adjoint_real, adjoint_imag], axis=0), fold_columns)
    real, imag = folded[:KR], folded[KR:]
    even = lanes((KR, 2 * KC)) <= HALF
    kinds = jnp.concatenate([jnp.where(even, real, imag), jnp.where(even, -imag, real)], axis=0)
    packed = dot(fold_rows, kinds)
    last = dot_nt(pick, packed[:, KC:])
    return jnp.concatenate([packed[:KR, :KC], packed[KR : KR + 8, :KC] + last], axis=0)


def final_math(total, mask, rows, turn_cos, turn_sin, columns, last_column):
    part = dot(rows[:, :40], total)
    edge = jnp.sum(rows * total[KR + 1 : KR + 2], axis=1, keepdims=True)
    turned = part * turn_cos + roll(part, HALF) * turn_sin
    grad = dot(turned, columns) + edge * last_column
    opening = logistic(mask)
    return grad * opening * (1.0 - opening)


VMEM = pl.BlockSpec(memory_space=pltpu.VMEM)
SMEM = pl.BlockSpec(memory_space=pltpu.SMEM)


def call(body, outputs, name, scalars, arrays):
    arrays = [pltpu.with_memory_space_constraint(array, pltpu.VMEM) for array in arrays]
    return pl.pallas_call(
        body,
        in_specs=[SMEM] * len(scalars) + [VMEM] * len(arrays),
        out_specs=jax.tree.map(lambda _: VMEM, outputs),
        out_shape=outputs,
        name=name,
    )(*scalars, *arrays)


def plain(*shape):
    return jax.ShapeDtypeStruct(shape, jnp.float32)


def pick_block(table, index):
    return lax.dynamic_index_in_dim(jnp.asarray(table), index, 0, False)


def columns_part(row_index, mask_param, target):
    tables = (column_table(), *turn_tables(), fold_tables()[2])
    turn = own_row_table()
    if not KERNELS:
        message = jnp.concatenate(columns_math(mask_param, *tables))
        return repeated(message, ROW_BLOCKS), repeated(target, NEAR), pick_block(turn, row_index)

    def kernel(place, mask_ref, target_ref, turn_ref, *refs):
        *refs, out_ref, near_ref, own_ref = refs
        own_ref[...] = turn_ref[0]
        for b in range(NEAR):
            near_ref[b] = target_ref[...]
        main, edge = columns_math(mask_ref[...], *[ref[...] for ref in refs])
        for b in range(ROW_BLOCKS):
            out_ref[LINES * b : LINES * b + ROWS] = main
            out_ref[LINES * b + ROWS : LINES * (b + 1)] = edge

    full = lambda shape: pl.BlockSpec(shape, lambda i, place: (0,) * len(shape))
    outputs = (
        plain(ROW_BLOCKS * LINES, KC),
        jax.ShapeDtypeStruct((NEAR, *target.shape), target.dtype),
        plain(*turn.shape[1:]),
    )
    sent, near, own = pl.pallas_call(
        kernel,
        grid_spec=pltpu.PrefetchScalarGridSpec(
            num_scalar_prefetch=1,
            grid=(1,),
            in_specs=[
                full(mask_param.shape),
                full(target.shape),
                pl.BlockSpec((1, *turn.shape[1:]), lambda i, place: (place[0], 0, 0)),
                *[full(table.shape) for table in tables],
            ],
            out_specs=tuple(full(output.shape) for output in outputs),
        ),
        out_shape=outputs,
        name="columns_part",
    )(row_index.reshape(1), mask_param, target, turn, *tables)
    return sent.reshape(ROW_BLOCKS, 1, LINES * KC), near, own


def repeated(values, count):
    return jnp.broadcast_to(values[None], (count, *values.shape))


def field_part(half, weight, row_shift, col_shift, heard, turn):
    heard = heard.reshape(ROW_BLOCKS * LINES, KC)
    arrays = (
        heard,
        turn,
        *band_tables(),
        spread_table(),
        f32(sample_table()),
        f32(interpolation_table()),
    )
    scalars = (half.reshape(1), weight, row_shift, col_shift)
    if not KERNELS:
        lines = heard.reshape(ROW_BLOCKS, LINES, KC)
        main, edge = lines[:, :ROWS].reshape(NR, KC), lines[:, ROWS]
        return field_math(half, *scalars[1:], main, edge, *arrays[1:])

    def kernel(half_ref, weight_ref, row_ref, col_ref, heard_ref, *refs):
        *refs, field_ref, resist_ref = refs
        main = jnp.concatenate(
            [heard_ref[LINES * b : LINES * b + ROWS] for b in range(ROW_BLOCKS)], axis=0
        )
        edge = heard_ref[pl.ds(ROWS, ROW_BLOCKS, stride=LINES)]
        field_ref[...], resist_ref[...] = field_math(
            half_ref[0], weight_ref, row_ref, col_ref, main, edge, *[ref[...] for ref in refs]
        )

    outputs = (
        pltpu.VMEM((POINTS * ROWS, 2 * MC), jnp.float32),
        pltpu.VMEM((NEAR * ROWS, SHARE), jnp.float32),
    )
    return call(kernel, outputs, "field_part", scalars, arrays)


def adjoint_part(half, weight, row_shift, col_shift, target, resist, field, turn):
    arrays = (
        target.reshape(NEAR * ROWS, SHARE),
        resist,
        field,
        turn,
        f32(sample_table()),
        f32(interpolation_table()),
        *fold_tables(),
    )
    scalars = (half.reshape(1), weight, row_shift, col_shift)
    if not KERNELS:
        return repeated(adjoint_math(half, *scalars[1:], *arrays), 8)

    def kernel(half_ref, weight_ref, row_ref, col_ref, *refs):
        *refs, out_ref = refs
        message = adjoint_math(
            half_ref[0], weight_ref, row_ref, col_ref, *[ref[...] for ref in refs]
        )
        for b in range(8):
            out_ref[b] = message

    return call(kernel, plain(8, 40, KC), "adjoint_part", scalars, arrays)


def repeat_sum(received):
    if not KERNELS:
        return jnp.broadcast_to(jnp.sum(received, axis=0)[None], received.shape)

    def kernel(in_ref, out_ref):
        total = in_ref[0]
        for b in range(1, received.shape[0]):
            total = total + in_ref[b]
        for b in range(received.shape[0]):
            out_ref[b] = total

    return call(kernel, plain(*received.shape), "repeat_sum", (), (received,))


def final_part(src_index, row_index, received, mask_param):
    rows, columns, last_column = final_tables()
    arrays = (
        received,
        lax.dynamic_slice_in_dim(mask_param, src_index * SHARE, SHARE, 1),
        pick_block(rows, row_index),
        *[pick_block(table.reshape(BLOCKS, 1, KC), src_index) for table in turn_tables()],
        columns,
        last_column,
    )
    if not KERNELS:
        return final_math(jnp.sum(received, axis=0), *arrays[1:])

    def kernel(in_ref, *refs):
        *refs, out_ref = refs
        total = in_ref[0]
        for b in range(1, received.shape[0]):
            total = total + in_ref[b]
        out_ref[...] = final_math(total, *[ref[...] for ref in refs])

    return call(kernel, plain(ROWS, SHARE), "final_part", (), arrays)


def swap(values, axis):
    return lax.all_to_all(values, axis, 0, 0, tiled=True)


def local(mask_param, target, source_weight, row_shift, col_shift):
    half = lax.axis_index("zh")
    src_index = lax.axis_index(("zh", "x", "c"))
    row_index = lax.axis_index(("zl", "y"))
    source = (source_weight, row_shift, col_shift)
    sent, near, turn = columns_part(row_index, mask_param, target)
    heard = swap(sent, ("zl", "y"))
    near = swap(near, ("x", "c"))
    field, resist = field_part(half, *source, heard, turn)
    message = adjoint_part(half, *source, near, resist, field, turn)
    message = repeat_sum(swap(message, "y"))
    return final_part(src_index, row_index, swap(message, ("zh", "zl")), mask_param)


def solution(mesh):
    fine = Mesh(mesh.devices.reshape(2, 4, 2, 4, 8), ("zh", "x", "c", "zl", "y"))
    rows, src = ("zl", "y"), ("zh", "x", "c")
    placed = (P(rows, None), P(rows, src), P(), P(), P())
    return jax.shard_map(
        local, mesh=fine, in_specs=placed, out_specs=P(rows, src), check_vma=False
    )
```

```python
import math

import jax
import jax.numpy as jnp
import numpy as np
from jax import lax
from jax.experimental import pallas as pl
from jax.experimental.pallas import tpu as pltpu
from jax.sharding import Mesh
from jax.sharding import PartitionSpec as P


steepness = 250.0
threshold_level = 0.25
loss_weight = 8.0
highest = lax.Precision.HIGHEST
KERNELS = True

NR = 512
NC = 8192
KR = 32
KC = 128
MC = 256
HALF = KC // 2
SHARE = 512
BLOCKS = NC // SHARE
ROWS = 16
ROW_BLOCKS = NR // ROWS
POINTS = 16
NEAR = 8
STEP = MC // BLOCKS
LINES = ROWS + 1
UNIT = 1.0 / math.sqrt(NR * NC)


def f32(table):
    return np.ascontiguousarray(np.asarray(table, dtype=np.float32))


def wave(frequency, position, period):
    angle = (np.outer(frequency, position) % period) * (2.0 * np.pi / period)
    return np.cos(angle), np.sin(angle)


def column_table():
    cos, sin = wave(np.arange(HALF + 1), np.arange(SHARE), NC)
    table = np.zeros((2 * KC, SHARE))
    table[:HALF] = cos[:HALF]
    table[HALF] = cos[HALF]
    table[HALF + 1 : KC] = -sin[1:HALF]
    table[KC] = -sin[HALF]
    return f32(table[: KC + 8])


def turn_tables():
    cos, sin = wave(np.arange(BLOCKS), np.arange(HALF), BLOCKS)
    return f32(np.concatenate([cos, cos], axis=1)), f32(np.concatenate([sin, -sin], axis=1))


def spread_table():
    table = np.zeros((KC, 2 * KC))
    for frequency in range(-HALF, HALF):
        size, at = abs(frequency), frequency + HALF
        table[size, at] = 1.0
        if 0 < size < HALF:
            table[HALF + size, KC + at] = 1.0 if frequency > 0 else -1.0
    return f32(table)


def band_tables():
    frequency = np.arange(KR) - KR // 2
    rows = np.concatenate(wave(frequency, np.arange(NR), NR)) * (UNIT * UNIT)
    inner = np.zeros((2 * KR, KC))
    inner[:, :ROWS] = np.concatenate(wave(frequency, np.arange(ROWS), NR)) * (UNIT * UNIT)
    outer = np.concatenate(wave(frequency, np.arange(ROW_BLOCKS) * ROWS, NR))
    return f32(rows), f32(inner), f32(outer)


def own_row_table():
    cos, sin = wave(np.arange(NR), np.arange(KR) - KR // 2, NR)
    cos = cos.reshape(ROW_BLOCKS, ROWS, KR)
    sin = sin.reshape(ROW_BLOCKS, ROWS, KR)
    turn = np.concatenate(
        [np.concatenate([cos, -sin], axis=2), np.concatenate([sin, cos], axis=2)], axis=1
    )
    return f32(turn)


def sample_table():
    cos, sin = wave(np.arange(KC) - HALF, np.arange(MC), MC)
    return np.block([[cos, sin], [-sin, cos]])


def interpolation_table():
    place = (np.arange(MC)[:, None] * (NC // MC) - np.arange(SHARE)[None, :]) % NC
    total = np.ones_like(place, dtype=np.float64)
    for k in range(1, HALF + 1):
        total += 2.0 * np.cos(((place * k) % NC) * (2.0 * np.pi / NC))
    return total / MC


def fold_tables():
    columns = np.zeros((KC, 2 * KC))
    for frequency in range(-HALF, HALF):
        at, size = frequency + HALF, abs(frequency)
        columns[at, size] = 1.0
        if size > 0:
            columns[at, HALF + size] = -1.0 if frequency > 0 else 1.0
    columns[0, KC] = 1.0
    columns[0, HALF] = 1.0
    rows = np.zeros((KC, 2 * KR))
    for frequency in range(-KR // 2, KR // 2):
        at, size = frequency + KR // 2, abs(frequency)
        rows[size, at] = 1.0
        if size > 0:
            rows[KR // 2 + size, KR + at] = float(np.sign(frequency))
    pick = np.zeros((8, KC))
    pick[1, 0] = 1.0
    return f32(columns), f32(rows), f32(pick)


def final_tables():
    cos, sin = wave(np.arange(NR), np.arange(KR // 2 + 1), NR)
    rows = np.zeros((NR, KC))
    rows[:, : KR // 2 + 1] = cos * UNIT
    rows[:, KR // 2 + 1 : KR + 1] = sin[:, 1:] * UNIT
    cos_y, sin_y = wave(np.arange(HALF + 1), np.arange(SHARE), NC)
    columns = np.concatenate([cos_y, sin_y[1:HALF]])
    return f32(rows.reshape(ROW_BLOCKS, ROWS, KC)), f32(columns), f32(sin_y[HALF:])


def dot(left, right):
    return jnp.dot(left, right, precision=highest, preferred_element_type=jnp.float32)


def dot_nt(left, right, precision=highest):
    return lax.dot_general(
        left, right, (((1,), (1,)), ((), ())), precision=precision, preferred_element_type=jnp.float32
    )


def split(values):
    high = values.astype(jnp.bfloat16)
    return high, (values - high.astype(jnp.float32)).astype(jnp.bfloat16)


def dot3_nt(left, right):
    high, low = split(left)
    right_high, right_low = split(right)
    one = lambda a, b: dot_nt(a, b, None)
    return one(high, right_high) + (one(high, right_low) + one(low, right_high))


def dot_tn(left, right):
    return lax.dot_general(
        left, right, (((0,), (0,)), ((), ())), precision=highest, preferred_element_type=jnp.float32
    )


def logistic(values):
    return 1.0 / (1.0 + jnp.exp(-values))


def roll(values, shift):
    if KERNELS:
        return pltpu.roll(values, shift, axis=1)
    return jnp.roll(values, shift, axis=1)


def lanes(shape):
    return lax.broadcasted_iota(jnp.int32, shape, 1)


def columns_math(mask, base, turn_cos, turn_sin, pick):
    stacked = jnp.concatenate(
        [logistic(mask[:, SHARE * b : SHARE * (b + 1)]) for b in range(BLOCKS)], axis=0
    )
    parts = dot_nt(stacked, base)
    main = jnp.zeros((ROWS, KC), jnp.float32)
    edge = jnp.zeros((ROWS, 8), jnp.float32)
    for b in range(BLOCKS):
        part = parts[ROWS * b : ROWS * (b + 1)]
        first = part[:, :KC]
        main = main + first * turn_cos[b : b + 1] + roll(first, HALF) * turn_sin[b : b + 1]
        edge = edge + part[:, KC:]
    edge = jnp.concatenate([edge, jnp.zeros((KC - ROWS, 8), jnp.float32)], axis=0)
    return main, dot_nt(pick[:, :8], edge)[1:2]


def pupil(row_shift, col_shift):
    radius_rows = KR // 4
    radius_cols = KC // 4
    fr = lax.broadcasted_iota(jnp.int32, (KR, KC), 0) - KR // 2 + row_shift
    fc = lanes((KR, KC)) - HALF + col_shift
    limit_value = (radius_rows * radius_cols) ** 2
    inside = fr * fr * (radius_cols * radius_cols) + fc * fc * (radius_rows * radius_rows)
    return (inside <= limit_value).astype(jnp.float32)


def middle_math(
    shifts,
    weight,
    row_shift,
    col_shift,
    main,
    edge,
    target,
    turn,
    rows,
    inner,
    outer,
    spread,
    to_samples,
    interpolate,
    fold_columns,
    fold_rows,
    pick,
):
    both = dot(dot(rows, main), spread)
    inside = dot_nt(inner, edge)
    in_cos, in_sin = inside[:KR], inside[KR:]
    out_cos, out_sin = outer[:KR], outer[KR:]
    edge_cos = jnp.sum(out_cos * in_cos - out_sin * in_sin, axis=1, keepdims=True)
    edge_sin = jnp.sum(out_sin * in_cos + out_cos * in_sin, axis=1, keepdims=True)
    edge_column = jnp.concatenate([edge_cos, edge_sin], axis=0)
    real = both[:, :KC]
    imag = both[:, KC:] - jnp.where(lanes((2 * KR, KC)) == 0, edge_column, 0.0)
    band_real = real[:KR] + imag[KR:]
    band_imag = imag[:KR] - real[KR:]

    opened = [pupil(row_shift[s], col_shift[s]) for s in range(POINTS)]
    masked = jnp.concatenate(
        [
            jnp.concatenate([band_real * opened[s], band_imag * opened[s]], axis=0)
            for s in range(POINTS)
        ],
        axis=1,
    )
    head = dot(turn, masked)
    head = jnp.concatenate(
        [
            jnp.concatenate(
                [head[:ROWS, KC * s : KC * (s + 1)], head[ROWS:, KC * s : KC * (s + 1)]], axis=1
            )
            for s in range(POINTS)
        ],
        axis=0,
    )
    field = dot(head, to_samples)
    samples = jnp.zeros((ROWS, MC), jnp.float32)
    total = 0.0
    for s in range(POINTS):
        now = field[ROWS * s : ROWS * (s + 1)]
        samples = samples + weight[s] * (now[:, :MC] * now[:, :MC] + now[:, MC:] * now[:, MC:])
        total = total + weight[s]
    share = 1.0 / jnp.full((ROWS, MC), total, jnp.float32)
    samples = samples * share
    near = jnp.concatenate(
        [roll(samples, (MC - shifts[j]) & (MC - 1)) for j in range(NEAR)], axis=0
    )
    intensity = dot(near, interpolate)
    resist = logistic(steepness * (intensity - threshold_level))
    slope = (
        2.0
        * loss_weight
        * (resist - target.astype(jnp.float32))
        * steepness
        * resist
        * (1.0 - resist)
    )
    lows = dot3_nt(slope, interpolate)
    low = roll(lows[:ROWS], shifts[0])
    for j in range(1, NEAR):
        low = low + roll(lows[ROWS * j : ROWS * (j + 1)], shifts[j])
    low = low * share * (2.0 * UNIT)
    wide = jnp.concatenate([low, low], axis=1)
    scaled = jnp.concatenate(
        [(weight[s] * wide) * field[ROWS * s : ROWS * (s + 1)] for s in range(POINTS)], axis=0
    )
    back = dot3_nt(scaled, to_samples)
    back = jnp.concatenate(
        [
            jnp.concatenate(
                [back[ROWS * s : ROWS * (s + 1), :KC], back[ROWS * s : ROWS * (s + 1), KC:]], axis=0
            )
            for s in range(POINTS)
        ],
        axis=1,
    )
    spectra = dot_tn(turn, back)
    adjoint_real = jnp.zeros((KR, KC), jnp.float32)
    adjoint_imag = jnp.zeros((KR, KC), jnp.float32)
    for s in range(POINTS):
        now = spectra[:, KC * s : KC * (s + 1)]
        adjoint_real = adjoint_real + opened[s] * now[:KR]
        adjoint_imag = adjoint_imag + opened[s] * now[KR:]
    folded = dot(jnp.concatenate([adjoint_real, adjoint_imag], axis=0), fold_columns)
    real, imag = folded[:KR], folded[KR:]
    even = lanes((KR, 2 * KC)) <= HALF
    kinds = jnp.concatenate([jnp.where(even, real, imag), jnp.where(even, -imag, real)], axis=0)
    packed = dot(fold_rows, kinds)
    last = dot_nt(pick, packed[:, KC:])
    return jnp.concatenate([packed[:KR, :KC], packed[KR : KR + 8, :KC] + last], axis=0)


def final_math(total, mask, rows, turn_cos, turn_sin, columns, last_column):
    part = dot(rows[:, :40], total)
    edge = jnp.sum(rows * total[KR + 1 : KR + 2], axis=1, keepdims=True)
    turned = part * turn_cos + roll(part, HALF) * turn_sin
    grad = dot(turned, columns) + edge * last_column
    opening = logistic(mask)
    return grad * opening * (1.0 - opening)


VMEM = pl.BlockSpec(memory_space=pltpu.VMEM)
SMEM = pl.BlockSpec(memory_space=pltpu.SMEM)


def call(body, outputs, scalars, arrays):
    arrays = [pltpu.with_memory_space_constraint(array, pltpu.VMEM) for array in arrays]
    return pl.pallas_call(
        body,
        in_specs=[SMEM] * len(scalars) + [VMEM] * len(arrays),
        out_specs=jax.tree.map(lambda _: VMEM, outputs),
        out_shape=outputs,
    )(*scalars, *arrays)


def plain(*shape):
    return jax.ShapeDtypeStruct(shape, jnp.float32)


def pick_block(table, index):
    return lax.dynamic_index_in_dim(jnp.asarray(table), index, 0, False)


def columns_part(row_index, mask_param):
    tables = (column_table(), *turn_tables(), fold_tables()[2])
    turn = own_row_table()
    if not KERNELS:
        message = jnp.concatenate(columns_math(mask_param, *tables))
        return repeated(message, ROW_BLOCKS), pick_block(turn, row_index)

    def kernel(place, mask_ref, turn_ref, *refs):
        *refs, out_ref, own_ref = refs
        own_ref[...] = turn_ref[0]
        main, edge = columns_math(mask_ref[...], *[ref[...] for ref in refs])
        for b in range(ROW_BLOCKS):
            out_ref[LINES * b : LINES * b + ROWS] = main
            out_ref[LINES * b + ROWS : LINES * (b + 1)] = edge

    full = lambda shape: pl.BlockSpec(shape, lambda i, place: (0,) * len(shape))
    outputs = (
        pltpu.VMEM((ROW_BLOCKS * LINES, KC), jnp.float32),
        pltpu.VMEM(turn.shape[1:], jnp.float32),
    )
    sent, own = pl.pallas_call(
        kernel,
        grid_spec=pltpu.PrefetchScalarGridSpec(
            num_scalar_prefetch=1,
            grid=(1,),
            in_specs=[
                full(mask_param.shape),
                pl.BlockSpec((1, *turn.shape[1:]), lambda i, place: (place[0], 0, 0)),
                *[full(table.shape) for table in tables],
            ],
            out_specs=tuple(full(output.shape) for output in outputs),
        ),
        out_shape=outputs,
        name="columns_part",
    )(row_index.reshape(1), mask_param, turn, *tables)
    return sent.reshape(ROW_BLOCKS, 1, LINES * KC), own


def repeated(values, count):
    return jnp.broadcast_to(values[None], (count, *values.shape))


def middle_part(shifts, weight, row_shift, col_shift, heard, targets, turn):
    heard = heard.reshape(ROW_BLOCKS * LINES, KC)
    targets = [target.reshape(-1, SHARE) for target in targets]
    arrays = (
        heard,
        *targets,
        turn,
        *band_tables(),
        spread_table(),
        f32(sample_table()),
        f32(interpolation_table()),
        *fold_tables(),
    )
    scalars = (shifts, weight, row_shift, col_shift)
    if not KERNELS:
        lines = heard.reshape(ROW_BLOCKS, LINES, KC)
        main, edge = lines[:, :ROWS].reshape(NR, KC), lines[:, ROWS]
        target = jnp.concatenate(targets)
        return repeated(middle_math(*scalars, main, edge, target, *arrays[1 + len(targets) :]), 8)

    def kernel(shift_ref, weight_ref, row_ref, col_ref, heard_ref, *refs):
        *refs, out_ref = refs
        main = jnp.concatenate(
            [heard_ref[LINES * b : LINES * b + ROWS] for b in range(ROW_BLOCKS)], axis=0
        )
        edge = heard_ref[pl.ds(ROWS, ROW_BLOCKS, stride=LINES)]
        values = [ref[...] for ref in refs]
        target = jnp.concatenate(values[: len(targets)], axis=0)
        message = middle_math(
            shift_ref, weight_ref, row_ref, col_ref, main, edge, target, *values[len(targets) :]
        )
        for b in range(8):
            out_ref[b] = message

    return call(kernel, plain(8, 40, KC), scalars, arrays)


def repeat_sum(received):
    if not KERNELS:
        return jnp.broadcast_to(jnp.sum(received, axis=0)[None], received.shape)

    def kernel(in_ref, out_ref):
        total = in_ref[0]
        for b in range(1, received.shape[0]):
            total = total + in_ref[b]
        for b in range(received.shape[0]):
            out_ref[b] = total

    return call(kernel, pltpu.VMEM(received.shape, jnp.float32), (), (received,))


def final_part(src_index, row_index, received, mask_param):
    rows, columns, last_column = final_tables()
    arrays = (
        received,
        lax.dynamic_slice_in_dim(mask_param, src_index * SHARE, SHARE, 1),
        pick_block(rows, row_index),
        *[pick_block(table.reshape(BLOCKS, 1, KC), src_index) for table in turn_tables()],
        columns,
        last_column,
    )
    if not KERNELS:
        return final_math(jnp.sum(received, axis=0), *arrays[1:])

    def kernel(in_ref, *refs):
        *refs, out_ref = refs
        total = in_ref[0]
        for b in range(1, received.shape[0]):
            total = total + in_ref[b]
        out_ref[...] = final_math(total, *[ref[...] for ref in refs])

    return call(kernel, plain(ROWS, SHARE), (), arrays)


def swap(values, axis):
    return lax.all_to_all(values, axis, 0, 0, tiled=True)


def local(mask_param, target, source_weight, row_shift, col_shift):
    half, at, core = (lax.axis_index(name) for name in ("zh", "x", "c"))
    src_index = lax.axis_index(("zh", "x", "c"))
    row_index = lax.axis_index(("zl", "y"))
    places = [at, at ^ 1, 3 - at, (3 - at) ^ 1]
    shares = jnp.stack([2 * place + side for place in places for side in (core, 1 - core)])
    shifts = half * (MC // 2) + STEP * shares
    other = lax.ppermute(target, "c", [(0, 1), (1, 0)])
    sent, turn = columns_part(row_index, mask_param)
    two = jnp.stack([target, other])
    second = lax.ppermute(two, "x", [(i, i ^ 1) for i in range(4)])
    heard = swap(sent, ("zl", "y"))
    four = jnp.concatenate([two, second])
    third = lax.ppermute(four, "x", [(i, 3 - i) for i in range(4)])
    targets = (two, second, third)
    message = middle_part(shifts, source_weight, row_shift, col_shift, heard, targets, turn)
    message = repeat_sum(swap(message, "y"))
    return final_part(src_index, row_index, swap(message, ("zh", "zl")), mask_param)


def solution(mesh):
    fine = Mesh(mesh.devices.reshape(2, 4, 2, 4, 8), ("zh", "x", "c", "zl", "y"))
    rows, src = ("zl", "y"), ("zh", "x", "c")
    placed = (P(rows, None), P(rows, src), P(), P(), P())
    return jax.shard_map(
        local, mesh=fine, in_specs=placed, out_specs=P(rows, src), check_vma=False
    )
```

```python
import math

import jax
import jax.numpy as jnp
import numpy as np
from jax import lax
from jax.experimental import pallas as pl
from jax.experimental.pallas import tpu as pltpu
from jax.sharding import Mesh
from jax.sharding import PartitionSpec as P


steepness = 250.0
threshold_level = 0.25
loss_weight = 8.0
highest = lax.Precision.HIGHEST
KERNELS = True

NR = 512
NC = 8192
KR = 32
KC = 128
MC = 256
HALF = KC // 2
SHARE = 512
BLOCKS = NC // SHARE
ROWS = 16
ROW_BLOCKS = NR // ROWS
POINTS = 16
NEAR = 8
STEP = MC // BLOCKS
LINES = ROWS + 1
ROW_ORDER = None
Y_ORDER = [4, 5, 6, 7, 0, 1, 2, 3]
Z_ORDER = [4, 5, 6, 7, 0, 1, 2, 3]
UNIT = 1.0 / math.sqrt(NR * NC)


def f32(table):
    return np.ascontiguousarray(np.asarray(table, dtype=np.float32))


def wave(frequency, position, period):
    angle = (np.outer(frequency, position) % period) * (2.0 * np.pi / period)
    return np.cos(angle), np.sin(angle)


def column_table():
    cos, sin = wave(np.arange(HALF + 1), np.arange(SHARE), NC)
    table = np.zeros((2 * KC, SHARE))
    table[:HALF] = cos[:HALF]
    table[HALF] = cos[HALF]
    table[HALF + 1 : KC] = -sin[1:HALF]
    table[KC] = -sin[HALF]
    return f32(table[: KC + 8])


def turn_tables():
    cos, sin = wave(np.arange(BLOCKS), np.arange(HALF), BLOCKS)
    return f32(np.concatenate([cos, cos], axis=1)), f32(np.concatenate([sin, -sin], axis=1))


def spread_table():
    table = np.zeros((KC, 2 * KC))
    for frequency in range(-HALF, HALF):
        size, at = abs(frequency), frequency + HALF
        table[size, at] = 1.0
        if 0 < size < HALF:
            table[HALF + size, KC + at] = 1.0 if frequency > 0 else -1.0
    return f32(table)


def band_tables():
    frequency = np.arange(KR) - KR // 2
    rows = np.concatenate(wave(frequency, np.arange(NR), NR)) * (UNIT * UNIT)
    inner = np.zeros((2 * KR, KC))
    inner[:, :ROWS] = np.concatenate(wave(frequency, np.arange(ROWS), NR)) * (UNIT * UNIT)
    outer = np.concatenate(wave(frequency, np.arange(ROW_BLOCKS) * ROWS, NR))
    return f32(rows), f32(inner), f32(outer)


def own_row_table():
    cos, sin = wave(np.arange(NR), np.arange(KR) - KR // 2, NR)
    cos = cos.reshape(ROW_BLOCKS, ROWS, KR)
    sin = sin.reshape(ROW_BLOCKS, ROWS, KR)
    turn = np.concatenate(
        [np.concatenate([cos, -sin], axis=2), np.concatenate([sin, cos], axis=2)], axis=1
    )
    return f32(turn)


def sample_table():
    cos, sin = wave(np.arange(KC) - HALF, np.arange(MC), MC)
    return np.block([[cos, sin], [-sin, cos]])


def interpolation_table():
    place = (np.arange(MC)[:, None] * (NC // MC) - np.arange(SHARE)[None, :]) % NC
    total = np.ones_like(place, dtype=np.float64)
    for k in range(1, HALF + 1):
        total += 2.0 * np.cos(((place * k) % NC) * (2.0 * np.pi / NC))
    return total / MC


def fold_tables():
    columns = np.zeros((KC, 2 * KC))
    for frequency in range(-HALF, HALF):
        at, size = frequency + HALF, abs(frequency)
        columns[at, size] = 1.0
        if size > 0:
            columns[at, HALF + size] = -1.0 if frequency > 0 else 1.0
    columns[0, KC] = 1.0
    columns[0, HALF] = 1.0
    rows = np.zeros((KC, 2 * KR))
    for frequency in range(-KR // 2, KR // 2):
        at, size = frequency + KR // 2, abs(frequency)
        rows[size, at] = 1.0
        if size > 0:
            rows[KR // 2 + size, KR + at] = float(np.sign(frequency))
    pick = np.zeros((8, KC))
    pick[1, 0] = 1.0
    return f32(columns), f32(rows), f32(pick)


def final_tables():
    cos, sin = wave(np.arange(NR), np.arange(KR // 2 + 1), NR)
    rows = np.zeros((NR, KC))
    rows[:, : KR // 2 + 1] = cos * UNIT
    rows[:, KR // 2 + 1 : KR + 1] = sin[:, 1:] * UNIT
    cos_y, sin_y = wave(np.arange(HALF + 1), np.arange(SHARE), NC)
    columns = np.concatenate([cos_y, sin_y[1:HALF]])
    return f32(rows.reshape(ROW_BLOCKS, ROWS, KC)), f32(columns), f32(sin_y[HALF:])


def dot(left, right):
    return jnp.dot(left, right, precision=highest, preferred_element_type=jnp.float32)


def dot_nt(left, right, precision=highest):
    return lax.dot_general(
        left, right, (((1,), (1,)), ((), ())), precision=precision, preferred_element_type=jnp.float32
    )


def split(values):
    high = values.astype(jnp.bfloat16)
    return high, (values - high.astype(jnp.float32)).astype(jnp.bfloat16)


def dot3_nt(left, right):
    high, low = split(left)
    right_high, right_low = split(right)
    one = lambda a, b: dot_nt(a, b, None)
    return one(high, right_high) + (one(high, right_low) + one(low, right_high))


def dot3_tn(left, right):
    left_high, left_low = split(left)
    right_high, right_low = split(right)
    one = lambda a, b: lax.dot_general(
        a, b, (((0,), (0,)), ((), ())), preferred_element_type=jnp.float32
    )
    return one(left_high, right_high) + (one(left_high, right_low) + one(left_low, right_high))


def dot_signs(left, right, signs_left):
    one = lambda a, b: jnp.dot(a, b, preferred_element_type=jnp.float32)
    values, signs = (right, left) if signs_left else (left, right)
    signs = signs.astype(jnp.bfloat16)
    total = None
    for part in split3(values):
        now = one(signs, part) if signs_left else one(part, signs)
        total = now if total is None else total + now
    return total


def split3(values):
    high, low = split(values)
    rest = values - high.astype(jnp.float32) - low.astype(jnp.float32)
    return high, low, rest.astype(jnp.bfloat16)


def logistic(values):
    return 1.0 / (1.0 + jnp.exp(-values))


def roll(values, shift):
    if KERNELS:
        return pltpu.roll(values, shift, axis=1)
    return jnp.roll(values, shift, axis=1)


def lanes(shape):
    return lax.broadcasted_iota(jnp.int32, shape, 1)


def columns_math(mask, base, turn_cos, turn_sin, pick):
    stacked = jnp.concatenate(
        [logistic(mask[:, SHARE * b : SHARE * (b + 1)]) for b in range(BLOCKS)], axis=0
    )
    parts = dot_nt(stacked, base)
    main = jnp.zeros((ROWS, KC), jnp.float32)
    edge = jnp.zeros((ROWS, 8), jnp.float32)
    for b in range(BLOCKS):
        part = parts[ROWS * b : ROWS * (b + 1)]
        first = part[:, :KC]
        main = main + first * turn_cos[b : b + 1] + roll(first, HALF) * turn_sin[b : b + 1]
        edge = edge + part[:, KC:]
    edge = jnp.concatenate([edge, jnp.zeros((KC - ROWS, 8), jnp.float32)], axis=0)
    return main, dot_nt(pick[:, :8], edge)[1:2]


def pupil(row_shift, col_shift):
    radius_rows = KR // 4
    radius_cols = KC // 4
    fr = lax.broadcasted_iota(jnp.int32, (KR, KC), 0) - KR // 2 + row_shift
    fc = lanes((KR, KC)) - HALF + col_shift
    limit_value = (radius_rows * radius_cols) ** 2
    inside = fr * fr * (radius_cols * radius_cols) + fc * fc * (radius_rows * radius_rows)
    return (inside <= limit_value).astype(jnp.float32)


def middle_math(
    shifts,
    weight,
    row_shift,
    col_shift,
    main,
    edge,
    target,
    turn,
    rows,
    inner,
    outer,
    spread,
    to_samples,
    interpolate,
    fold_columns,
    fold_rows,
    pick,
):
    both = dot_signs(dot(rows, main), spread, False)
    inside = dot_nt(inner, edge)
    in_cos, in_sin = inside[:KR], inside[KR:]
    out_cos, out_sin = outer[:KR], outer[KR:]
    edge_cos = jnp.sum(out_cos * in_cos - out_sin * in_sin, axis=1, keepdims=True)
    edge_sin = jnp.sum(out_sin * in_cos + out_cos * in_sin, axis=1, keepdims=True)
    edge_column = jnp.concatenate([edge_cos, edge_sin], axis=0)
    real = both[:, :KC]
    imag = both[:, KC:] - jnp.where(lanes((2 * KR, KC)) == 0, edge_column, 0.0)
    band_real = real[:KR] + imag[KR:]
    band_imag = imag[:KR] - real[KR:]

    opened = [pupil(row_shift[s], col_shift[s]) for s in range(POINTS)]
    masked = jnp.concatenate(
        [
            jnp.concatenate([band_real * opened[s], band_imag * opened[s]], axis=0)
            for s in range(POINTS)
        ],
        axis=1,
    )
    head = dot(turn, masked)
    head = jnp.concatenate(
        [
            jnp.concatenate(
                [head[:ROWS, KC * s : KC * (s + 1)], head[ROWS:, KC * s : KC * (s + 1)]], axis=1
            )
            for s in range(POINTS)
        ],
        axis=0,
    )
    field = dot(head, to_samples)
    samples = jnp.zeros((ROWS, MC), jnp.float32)
    total = 0.0
    for s in range(POINTS):
        now = field[ROWS * s : ROWS * (s + 1)]
        samples = samples + weight[s] * (now[:, :MC] * now[:, :MC] + now[:, MC:] * now[:, MC:])
        total = total + weight[s]
    share = 1.0 / jnp.full((ROWS, MC), total, jnp.float32)
    samples = samples * share
    near = jnp.concatenate(
        [roll(samples, (MC - shifts[j]) & (MC - 1)) for j in range(NEAR)], axis=0
    )
    intensity = dot(near, interpolate)
    resist = logistic(steepness * (intensity - threshold_level))
    slope = (
        2.0
        * loss_weight
        * (resist - target.astype(jnp.float32))
        * steepness
        * resist
        * (1.0 - resist)
    )
    lows = dot3_nt(slope, interpolate)
    low = roll(lows[:ROWS], shifts[0])
    for j in range(1, NEAR):
        low = low + roll(lows[ROWS * j : ROWS * (j + 1)], shifts[j])
    low = low * share * (2.0 * UNIT)
    wide = jnp.concatenate([low, low], axis=1)
    scaled = jnp.concatenate(
        [(weight[s] * wide) * field[ROWS * s : ROWS * (s + 1)] for s in range(POINTS)], axis=0
    )
    back = dot3_nt(scaled, to_samples)
    back = jnp.concatenate(
        [
            jnp.concatenate(
                [back[ROWS * s : ROWS * (s + 1), :KC], back[ROWS * s : ROWS * (s + 1), KC:]], axis=0
            )
            for s in range(POINTS)
        ],
        axis=1,
    )
    spectra = dot3_tn(turn, back)
    adjoint_real = jnp.zeros((KR, KC), jnp.float32)
    adjoint_imag = jnp.zeros((KR, KC), jnp.float32)
    for s in range(POINTS):
        now = spectra[:, KC * s : KC * (s + 1)]
        adjoint_real = adjoint_real + opened[s] * now[:KR]
        adjoint_imag = adjoint_imag + opened[s] * now[KR:]
    folded = dot_signs(
        jnp.concatenate([adjoint_real, adjoint_imag], axis=0), fold_columns, False
    )
    real, imag = folded[:KR], folded[KR:]
    even = lanes((KR, 2 * KC)) <= HALF
    kinds = jnp.concatenate([jnp.where(even, real, imag), jnp.where(even, -imag, real)], axis=0)
    packed = dot_signs(fold_rows, kinds, True)
    last = dot_nt(pick, packed[:, KC:])
    return jnp.concatenate([packed[:KR, :KC], packed[KR : KR + 8, :KC] + last], axis=0)


def final_math(total, mask, rows, turn_cos, turn_sin, columns, last_column):
    part = dot(rows[:, :40], total)
    edge = jnp.sum(rows * total[KR + 1 : KR + 2], axis=1, keepdims=True)
    turned = part * turn_cos + roll(part, HALF) * turn_sin
    grad = dot(turned, columns) + edge * last_column
    opening = logistic(mask)
    return grad * opening * (1.0 - opening)


VMEM = pl.BlockSpec(memory_space=pltpu.VMEM)
SMEM = pl.BlockSpec(memory_space=pltpu.SMEM)


def call(body, outputs, scalars, arrays):
    arrays = [pltpu.with_memory_space_constraint(array, pltpu.VMEM) for array in arrays]
    return pl.pallas_call(
        body,
        in_specs=[SMEM] * len(scalars) + [VMEM] * len(arrays),
        out_specs=jax.tree.map(lambda _: VMEM, outputs),
        out_shape=outputs,
    )(*scalars, *arrays)


def plain(*shape):
    return jax.ShapeDtypeStruct(shape, jnp.float32)


def pick_block(table, index):
    return lax.dynamic_index_in_dim(jnp.asarray(table), index, 0, False)


def columns_part(row_index, mask_param):
    tables = (column_table(), *turn_tables(), fold_tables()[2])
    turn = own_row_table()
    if not KERNELS:
        message = jnp.concatenate(columns_math(mask_param, *tables))
        return repeated(message, ROW_BLOCKS), pick_block(turn, row_index)

    def kernel(place, mask_ref, turn_ref, *refs):
        *refs, out_ref, own_ref = refs
        own_ref[...] = turn_ref[0]
        main, edge = columns_math(mask_ref[...], *[ref[...] for ref in refs])
        for b in range(ROW_BLOCKS):
            out_ref[LINES * b : LINES * b + ROWS] = main
            out_ref[LINES * b + ROWS : LINES * (b + 1)] = edge

    full = lambda shape: pl.BlockSpec(shape, lambda i, place: (0,) * len(shape))
    outputs = (
        pltpu.VMEM((ROW_BLOCKS * LINES, KC), jnp.float32),
        pltpu.VMEM(turn.shape[1:], jnp.float32),
    )
    sent, own = pl.pallas_call(
        kernel,
        grid_spec=pltpu.PrefetchScalarGridSpec(
            num_scalar_prefetch=1,
            grid=(1,),
            in_specs=[
                full(mask_param.shape),
                pl.BlockSpec((1, *turn.shape[1:]), lambda i, place: (place[0], 0, 0)),
                *[full(table.shape) for table in tables],
            ],
            out_specs=tuple(full(output.shape) for output in outputs),
        ),
        out_shape=outputs,
        name="columns_part",
    )(row_index.reshape(1), mask_param, turn, *tables)
    return sent.reshape(ROW_BLOCKS, 1, LINES * KC), own


def repeated(values, count):
    return jnp.broadcast_to(values[None], (count, *values.shape))


def middle_part(shifts, weight, row_shift, col_shift, heard, targets, turn):
    heard = heard.reshape(ROW_BLOCKS * LINES, KC)
    targets = [target.reshape(-1, SHARE) for target in targets]
    arrays = (
        heard,
        *targets,
        turn,
        *band_tables(),
        spread_table(),
        f32(sample_table()),
        f32(interpolation_table()),
        *fold_tables(),
    )
    scalars = (shifts, weight, row_shift, col_shift)
    if not KERNELS:
        lines = heard.reshape(ROW_BLOCKS, LINES, KC)
        main, edge = lines[:, :ROWS].reshape(NR, KC), lines[:, ROWS]
        target = jnp.concatenate(targets)
        return repeated(middle_math(*scalars, main, edge, target, *arrays[1 + len(targets) :]), 8)

    def kernel(shift_ref, weight_ref, row_ref, col_ref, heard_ref, *refs):
        *refs, out_ref = refs
        main = jnp.concatenate(
            [heard_ref[LINES * b : LINES * b + ROWS] for b in range(ROW_BLOCKS)], axis=0
        )
        edge = heard_ref[pl.ds(ROWS, ROW_BLOCKS, stride=LINES)]
        values = [ref[...] for ref in refs]
        target = jnp.concatenate(values[: len(targets)], axis=0)
        message = middle_math(
            shift_ref, weight_ref, row_ref, col_ref, main, edge, target, *values[len(targets) :]
        )
        for b in range(8):
            out_ref[b] = message

    return call(kernel, plain(8, 40, KC), scalars, arrays)


def repeat_sum(received):
    if not KERNELS:
        return jnp.broadcast_to(jnp.sum(received, axis=0)[None], received.shape)

    def kernel(in_ref, out_ref):
        total = in_ref[0]
        for b in range(1, received.shape[0]):
            total = total + in_ref[b]
        for b in range(received.shape[0]):
            out_ref[b] = total

    return call(kernel, pltpu.VMEM(received.shape, jnp.float32), (), (received,))


def final_part(src_index, row_index, received, mask_param):
    rows, columns, last_column = final_tables()
    arrays = (
        received,
        lax.dynamic_slice_in_dim(mask_param, src_index * SHARE, SHARE, 1),
        pick_block(rows, row_index),
        *[pick_block(table.reshape(BLOCKS, 1, KC), src_index) for table in turn_tables()],
        columns,
        last_column,
    )
    if not KERNELS:
        return final_math(jnp.sum(received, axis=0), *arrays[1:])

    def kernel(in_ref, *refs):
        *refs, out_ref = refs
        total = in_ref[0]
        for b in range(1, received.shape[0]):
            total = total + in_ref[b]
        out_ref[...] = final_math(total, *[ref[...] for ref in refs])

    return call(kernel, plain(ROWS, SHARE), (), arrays)


def swap(values, axis, order=None):
    groups = None if order is None else [order]
    return lax.all_to_all(values, axis, 0, 0, axis_index_groups=groups, tiled=True)


def local(mask_param, target, source_weight, row_shift, col_shift):
    half, at, core = (lax.axis_index(name) for name in ("zh", "x", "c"))
    src_index = lax.axis_index(("zh", "x", "c"))
    row_index = lax.axis_index(("zl", "y"))
    places = [at, at ^ 1, 3 - at, (3 - at) ^ 1]
    shares = jnp.stack([2 * place + side for place in places for side in (core, 1 - core)])
    shifts = half * (MC // 2) + STEP * shares
    other = lax.ppermute(target, "c", [(0, 1), (1, 0)])
    sent, turn = columns_part(row_index, mask_param)
    two = jnp.stack([target, other])
    second = lax.ppermute(two, "x", [(i, i ^ 1) for i in range(4)])
    heard = swap(sent, ("zl", "y"), ROW_ORDER)
    four = jnp.concatenate([two, second])
    third = lax.ppermute(four, "x", [(i, 3 - i) for i in range(4)])
    targets = (two, second, third)
    message = middle_part(shifts, source_weight, row_shift, col_shift, heard, targets, turn)
    message = repeat_sum(swap(message, "y", Y_ORDER))
    return final_part(src_index, row_index, swap(message, ("zh", "zl"), Z_ORDER), mask_param)


def solution(mesh):
    fine = Mesh(mesh.devices.reshape(2, 4, 2, 4, 8), ("zh", "x", "c", "zl", "y"))
    rows, src = ("zl", "y"), ("zh", "x", "c")
    placed = (P(rows, None), P(rows, src), P(), P(), P())
    return jax.shard_map(
        local, mesh=fine, in_specs=placed, out_specs=P(rows, src), check_vma=False
    )
```

```python
import math

import jax
import jax.numpy as jnp
import numpy as np
from jax import lax
from jax.experimental import pallas as pl
from jax.experimental.pallas import tpu as pltpu
from jax.sharding import Mesh
from jax.sharding import PartitionSpec as P


steepness = 250.0
threshold_level = 0.25
loss_weight = 8.0
highest = lax.Precision.HIGHEST
KERNELS = True

NR = 512
NC = 8192
KR = 32
KC = 128
MC = 256
HALF = KC // 2
SHARE = 512
BLOCKS = NC // SHARE
ROWS = 16
ROW_BLOCKS = NR // ROWS
POINTS = 16
NEAR = 8
STEP = MC // BLOCKS
LINES = ROWS + 1
ROW_ORDER = [(k + 12) % 32 for k in range(32)]
Y_ORDER = [4, 5, 6, 7, 0, 1, 2, 3]
Z_ORDER = [5, 6, 7, 0, 1, 2, 3, 4]
UNIT = 1.0 / math.sqrt(NR * NC)


def f32(table):
    return np.ascontiguousarray(np.asarray(table, dtype=np.float32))


def wave(frequency, position, period):
    angle = (np.outer(frequency, position) % period) * (2.0 * np.pi / period)
    return np.cos(angle), np.sin(angle)


def column_table():
    cos, sin = wave(np.arange(HALF + 1), np.arange(SHARE), NC)
    table = np.zeros((2 * KC, SHARE))
    table[:HALF] = cos[:HALF]
    table[HALF] = cos[HALF]
    table[HALF + 1 : KC] = -sin[1:HALF]
    table[KC] = -sin[HALF]
    return f32(table[: KC + 8])


def turn_tables():
    cos, sin = wave(np.arange(BLOCKS), np.arange(HALF), BLOCKS)
    return f32(np.concatenate([cos, cos], axis=1)), f32(np.concatenate([sin, -sin], axis=1))


def spread_table():
    table = np.zeros((KC, 2 * KC))
    for frequency in range(-HALF, HALF):
        size, at = abs(frequency), frequency + HALF
        table[size, at] = 1.0
        if 0 < size < HALF:
            table[HALF + size, KC + at] = 1.0 if frequency > 0 else -1.0
    return f32(table)


def band_tables():
    frequency = np.arange(KR) - KR // 2
    heard_rows = (np.array(ROW_ORDER)[:, None] * ROWS + np.arange(ROWS)).reshape(-1)
    rows = np.concatenate(wave(frequency, heard_rows, NR)) * (UNIT * UNIT)
    inner = np.zeros((2 * KR, KC))
    inner[:, :ROWS] = np.concatenate(wave(frequency, np.arange(ROWS), NR)) * (UNIT * UNIT)
    outer = np.concatenate(wave(frequency, np.array(ROW_ORDER) * ROWS, NR))
    return f32(rows), f32(inner), f32(outer)


def own_row_table():
    cos, sin = wave(np.arange(NR), np.arange(KR) - KR // 2, NR)
    cos = cos.reshape(ROW_BLOCKS, ROWS, KR)
    sin = sin.reshape(ROW_BLOCKS, ROWS, KR)
    turn = np.concatenate(
        [np.concatenate([cos, -sin], axis=2), np.concatenate([sin, cos], axis=2)], axis=1
    )
    return f32(turn)


def sample_table():
    cos, sin = wave(np.arange(KC) - HALF, np.arange(MC), MC)
    return np.block([[cos, sin], [-sin, cos]])


def interpolation_table():
    place = (np.arange(MC)[:, None] * (NC // MC) - np.arange(SHARE)[None, :]) % NC
    total = np.ones_like(place, dtype=np.float64)
    for k in range(1, HALF + 1):
        total += 2.0 * np.cos(((place * k) % NC) * (2.0 * np.pi / NC))
    return total / MC


def fold_tables():
    columns = np.zeros((KC, 2 * KC))
    for frequency in range(-HALF, HALF):
        at, size = frequency + HALF, abs(frequency)
        columns[at, size] = 1.0
        if size > 0:
            columns[at, HALF + size] = -1.0 if frequency > 0 else 1.0
    columns[0, KC] = 1.0
    columns[0, HALF] = 1.0
    rows = np.zeros((KC, 2 * KR))
    for frequency in range(-KR // 2, KR // 2):
        at, size = frequency + KR // 2, abs(frequency)
        rows[size, at] = 1.0
        if size > 0:
            rows[KR // 2 + size, KR + at] = float(np.sign(frequency))
    pick = np.zeros((8, KC))
    pick[1, 0] = 1.0
    return f32(columns), f32(rows), f32(pick)


def final_tables():
    cos, sin = wave(np.arange(NR), np.arange(KR // 2 + 1), NR)
    rows = np.zeros((NR, KC))
    rows[:, : KR // 2 + 1] = cos * UNIT
    rows[:, KR // 2 + 1 : KR + 1] = sin[:, 1:] * UNIT
    cos_y, sin_y = wave(np.arange(HALF + 1), np.arange(SHARE), NC)
    columns = np.concatenate([cos_y, sin_y[1:HALF]])
    return f32(rows.reshape(ROW_BLOCKS, ROWS, KC)), f32(columns), f32(sin_y[HALF:])


def dot(left, right):
    return jnp.dot(left, right, precision=highest, preferred_element_type=jnp.float32)


def dot_nt(left, right, precision=highest):
    return lax.dot_general(
        left, right, (((1,), (1,)), ((), ())), precision=precision, preferred_element_type=jnp.float32
    )


def split(values):
    high = values.astype(jnp.bfloat16)
    return high, (values - high.astype(jnp.float32)).astype(jnp.bfloat16)


def dot3_nt(left, right):
    high, low = split(left)
    right_high, right_low = split(right)
    one = lambda a, b: dot_nt(a, b, None)
    return one(high, right_high) + (one(high, right_low) + one(low, right_high))


def dot3_tn(left, right):
    left_high, left_low = split(left)
    right_high, right_low = split(right)
    one = lambda a, b: lax.dot_general(
        a, b, (((0,), (0,)), ((), ())), preferred_element_type=jnp.float32
    )
    return one(left_high, right_high) + (one(left_high, right_low) + one(left_low, right_high))


def dot_signs(left, right, signs_left):
    one = lambda a, b: jnp.dot(a, b, preferred_element_type=jnp.float32)
    values, signs = (right, left) if signs_left else (left, right)
    signs = signs.astype(jnp.bfloat16)
    total = None
    for part in split3(values):
        now = one(signs, part) if signs_left else one(part, signs)
        total = now if total is None else total + now
    return total


def split3(values):
    high, low = split(values)
    rest = values - high.astype(jnp.float32) - low.astype(jnp.float32)
    return high, low, rest.astype(jnp.bfloat16)


def logistic(values):
    return 1.0 / (1.0 + jnp.exp(-values))


def roll(values, shift):
    if KERNELS:
        return pltpu.roll(values, shift, axis=1)
    return jnp.roll(values, shift, axis=1)


def lanes(shape):
    return lax.broadcasted_iota(jnp.int32, shape, 1)


def columns_math(mask, base, turn_cos, turn_sin, pick):
    stacked = jnp.concatenate(
        [logistic(mask[:, SHARE * b : SHARE * (b + 1)]) for b in range(BLOCKS)], axis=0
    )
    parts = dot_nt(stacked, base)
    main = jnp.zeros((ROWS, KC), jnp.float32)
    edge = jnp.zeros((ROWS, 8), jnp.float32)
    for b in range(BLOCKS):
        part = parts[ROWS * b : ROWS * (b + 1)]
        first = part[:, :KC]
        main = main + first * turn_cos[b : b + 1] + roll(first, HALF) * turn_sin[b : b + 1]
        edge = edge + part[:, KC:]
    edge = jnp.concatenate([edge, jnp.zeros((KC - ROWS, 8), jnp.float32)], axis=0)
    return main, dot_nt(pick[:, :8], edge)[1:2]


def pupil(row_shift, col_shift):
    radius_rows = KR // 4
    radius_cols = KC // 4
    fr = lax.broadcasted_iota(jnp.int32, (KR, KC), 0) - KR // 2 + row_shift
    fc = lanes((KR, KC)) - HALF + col_shift
    limit_value = (radius_rows * radius_cols) ** 2
    inside = fr * fr * (radius_cols * radius_cols) + fc * fc * (radius_rows * radius_rows)
    return (inside <= limit_value).astype(jnp.float32)


def middle_math(
    shifts,
    weight,
    row_shift,
    col_shift,
    main,
    edge,
    target,
    turn,
    rows,
    inner,
    outer,
    spread,
    to_samples,
    interpolate,
    fold_columns,
    fold_rows,
    pick,
):
    both = dot_signs(dot(rows, main), spread, False)
    inside = dot_nt(inner, edge)
    in_cos, in_sin = inside[:KR], inside[KR:]
    out_cos, out_sin = outer[:KR], outer[KR:]
    edge_cos = jnp.sum(out_cos * in_cos - out_sin * in_sin, axis=1, keepdims=True)
    edge_sin = jnp.sum(out_sin * in_cos + out_cos * in_sin, axis=1, keepdims=True)
    edge_column = jnp.concatenate([edge_cos, edge_sin], axis=0)
    real = both[:, :KC]
    imag = both[:, KC:] - jnp.where(lanes((2 * KR, KC)) == 0, edge_column, 0.0)
    band_real = real[:KR] + imag[KR:]
    band_imag = imag[:KR] - real[KR:]

    opened = [pupil(row_shift[s], col_shift[s]) for s in range(POINTS)]
    masked = jnp.concatenate(
        [
            jnp.concatenate([band_real * opened[s], band_imag * opened[s]], axis=0)
            for s in range(POINTS)
        ],
        axis=1,
    )
    head = dot(turn, masked)
    head = jnp.concatenate(
        [
            jnp.concatenate(
                [head[:ROWS, KC * s : KC * (s + 1)], head[ROWS:, KC * s : KC * (s + 1)]], axis=1
            )
            for s in range(POINTS)
        ],
        axis=0,
    )
    field = dot(head, to_samples)
    samples = jnp.zeros((ROWS, MC), jnp.float32)
    total = 0.0
    for s in range(POINTS):
        now = field[ROWS * s : ROWS * (s + 1)]
        samples = samples + weight[s] * (now[:, :MC] * now[:, :MC] + now[:, MC:] * now[:, MC:])
        total = total + weight[s]
    share = 1.0 / jnp.full((ROWS, MC), total, jnp.float32)
    samples = samples * share
    near = jnp.concatenate(
        [roll(samples, (MC - shifts[j]) & (MC - 1)) for j in range(NEAR)], axis=0
    )
    intensity = dot(near, interpolate)
    resist = logistic(steepness * (intensity - threshold_level))
    slope = (
        2.0
        * loss_weight
        * (resist - target.astype(jnp.float32))
        * steepness
        * resist
        * (1.0 - resist)
    )
    lows = dot3_nt(slope, interpolate)
    low = roll(lows[:ROWS], shifts[0])
    for j in range(1, NEAR):
        low = low + roll(lows[ROWS * j : ROWS * (j + 1)], shifts[j])
    low = low * share * (2.0 * UNIT)
    wide = jnp.concatenate([low, low], axis=1)
    scaled = jnp.concatenate(
        [(weight[s] * wide) * field[ROWS * s : ROWS * (s + 1)] for s in range(POINTS)], axis=0
    )
    back = dot3_nt(scaled, to_samples)
    back = jnp.concatenate(
        [
            jnp.concatenate(
                [back[ROWS * s : ROWS * (s + 1), :KC], back[ROWS * s : ROWS * (s + 1), KC:]], axis=0
            )
            for s in range(POINTS)
        ],
        axis=1,
    )
    spectra = dot3_tn(turn, back)
    adjoint_real = jnp.zeros((KR, KC), jnp.float32)
    adjoint_imag = jnp.zeros((KR, KC), jnp.float32)
    for s in range(POINTS):
        now = spectra[:, KC * s : KC * (s + 1)]
        adjoint_real = adjoint_real + opened[s] * now[:KR]
        adjoint_imag = adjoint_imag + opened[s] * now[KR:]
    folded = dot_signs(
        jnp.concatenate([adjoint_real, adjoint_imag], axis=0), fold_columns, False
    )
    real, imag = folded[:KR], folded[KR:]
    even = lanes((KR, 2 * KC)) <= HALF
    kinds = jnp.concatenate([jnp.where(even, real, imag), jnp.where(even, -imag, real)], axis=0)
    packed = dot_signs(fold_rows, kinds, True)
    last = dot_nt(pick, packed[:, KC:])
    return jnp.concatenate([packed[:KR, :KC], packed[KR : KR + 8, :KC] + last], axis=0)


def final_math(total, mask, rows, turn_cos, turn_sin, columns, last_column):
    part = dot(rows[:, :40], total)
    edge = jnp.sum(rows * total[KR + 1 : KR + 2], axis=1, keepdims=True)
    turned = part * turn_cos + roll(part, HALF) * turn_sin
    grad = dot(turned, columns) + edge * last_column
    opening = logistic(mask)
    return grad * opening * (1.0 - opening)


VMEM = pl.BlockSpec(memory_space=pltpu.VMEM)
SMEM = pl.BlockSpec(memory_space=pltpu.SMEM)


def call(body, outputs, scalars, arrays):
    arrays = [pltpu.with_memory_space_constraint(array, pltpu.VMEM) for array in arrays]
    return pl.pallas_call(
        body,
        in_specs=[SMEM] * len(scalars) + [VMEM] * len(arrays),
        out_specs=jax.tree.map(lambda _: VMEM, outputs),
        out_shape=outputs,
    )(*scalars, *arrays)


def plain(*shape):
    return jax.ShapeDtypeStruct(shape, jnp.float32)


def pick_block(table, index):
    return lax.dynamic_index_in_dim(jnp.asarray(table), index, 0, False)


def columns_part(row_index, mask_param):
    tables = (column_table(), *turn_tables(), fold_tables()[2])
    turn = own_row_table()
    if not KERNELS:
        message = jnp.concatenate(columns_math(mask_param, *tables))
        return repeated(message, ROW_BLOCKS), pick_block(turn, row_index)

    def kernel(place, mask_ref, turn_ref, *refs):
        *refs, out_ref, own_ref = refs
        own_ref[...] = turn_ref[0]
        main, edge = columns_math(mask_ref[...], *[ref[...] for ref in refs])
        for b in range(ROW_BLOCKS):
            out_ref[LINES * b : LINES * b + ROWS] = main
            out_ref[LINES * b + ROWS : LINES * (b + 1)] = edge

    full = lambda shape: pl.BlockSpec(shape, lambda i, place: (0,) * len(shape))
    outputs = (
        pltpu.VMEM((ROW_BLOCKS * LINES, KC), jnp.float32),
        pltpu.VMEM(turn.shape[1:], jnp.float32),
    )
    sent, own = pl.pallas_call(
        kernel,
        grid_spec=pltpu.PrefetchScalarGridSpec(
            num_scalar_prefetch=1,
            grid=(1,),
            in_specs=[
                full(mask_param.shape),
                pl.BlockSpec((1, *turn.shape[1:]), lambda i, place: (place[0], 0, 0)),
                *[full(table.shape) for table in tables],
            ],
            out_specs=tuple(full(output.shape) for output in outputs),
        ),
        out_shape=outputs,
        name="columns_part",
    )(row_index.reshape(1), mask_param, turn, *tables)
    return sent.reshape(ROW_BLOCKS, 1, LINES * KC), own


def repeated(values, count):
    return jnp.broadcast_to(values[None], (count, *values.shape))


def middle_part(shifts, weight, row_shift, col_shift, heard, targets, turn):
    heard = heard.reshape(ROW_BLOCKS * LINES, KC)
    targets = [target.reshape(-1, SHARE) for target in targets]
    arrays = (
        heard,
        *targets,
        turn,
        *band_tables(),
        spread_table(),
        f32(sample_table()),
        f32(interpolation_table()),
        *fold_tables(),
    )
    scalars = (shifts, weight, row_shift, col_shift)
    if not KERNELS:
        lines = heard.reshape(ROW_BLOCKS, LINES, KC)
        main, edge = lines[:, :ROWS].reshape(NR, KC), lines[:, ROWS]
        target = jnp.concatenate(targets)
        return repeated(middle_math(*scalars, main, edge, target, *arrays[1 + len(targets) :]), 8)

    def kernel(shift_ref, weight_ref, row_ref, col_ref, heard_ref, *refs):
        *refs, out_ref = refs
        main = jnp.concatenate(
            [heard_ref[LINES * b : LINES * b + ROWS] for b in range(ROW_BLOCKS)], axis=0
        )
        edge = heard_ref[pl.ds(ROWS, ROW_BLOCKS, stride=LINES)]
        values = [ref[...] for ref in refs]
        target = jnp.concatenate(values[: len(targets)], axis=0)
        message = middle_math(
            shift_ref, weight_ref, row_ref, col_ref, main, edge, target, *values[len(targets) :]
        )
        for b in range(8):
            out_ref[b] = message

    return call(kernel, plain(8, 40, KC), scalars, arrays)


def repeat_sum(received):
    if not KERNELS:
        return jnp.broadcast_to(jnp.sum(received, axis=0)[None], received.shape)

    def kernel(in_ref, out_ref):
        total = in_ref[0]
        for b in range(1, received.shape[0]):
            total = total + in_ref[b]
        for b in range(received.shape[0]):
            out_ref[b] = total

    return call(kernel, pltpu.VMEM(received.shape, jnp.float32), (), (received,))


def final_part(src_index, row_index, received, mask_param):
    rows, columns, last_column = final_tables()
    arrays = (
        received,
        lax.dynamic_slice_in_dim(mask_param, src_index * SHARE, SHARE, 1),
        pick_block(rows, row_index),
        *[pick_block(table.reshape(BLOCKS, 1, KC), src_index) for table in turn_tables()],
        columns,
        last_column,
    )
    if not KERNELS:
        return final_math(jnp.sum(received, axis=0), *arrays[1:])

    def kernel(in_ref, *refs):
        *refs, out_ref = refs
        total = in_ref[0]
        for b in range(1, received.shape[0]):
            total = total + in_ref[b]
        out_ref[...] = final_math(total, *[ref[...] for ref in refs])

    return call(kernel, plain(ROWS, SHARE), (), arrays)


def swap(values, axis, order=None):
    groups = None if order is None else [order]
    return lax.all_to_all(values, axis, 0, 0, axis_index_groups=groups, tiled=True)


def local(mask_param, target, source_weight, row_shift, col_shift):
    half, at, core = (lax.axis_index(name) for name in ("zh", "x", "c"))
    src_index = lax.axis_index(("zh", "x", "c"))
    row_index = lax.axis_index(("zl", "y"))
    places = [at, at ^ 1, 3 - at, (3 - at) ^ 1]
    shares = jnp.stack([2 * place + side for place in places for side in (core, 1 - core)])
    shifts = half * (MC // 2) + STEP * shares
    other = lax.ppermute(target, "c", [(0, 1), (1, 0)])
    sent, turn = columns_part(row_index, mask_param)
    two = jnp.stack([target, other])
    second = lax.ppermute(two, "x", [(i, i ^ 1) for i in range(4)])
    heard = swap(sent, ("zl", "y"), ROW_ORDER)
    four = jnp.concatenate([two, second])
    third = lax.ppermute(four, "x", [(i, 3 - i) for i in range(4)])
    targets = (two, second, third)
    message = middle_part(shifts, source_weight, row_shift, col_shift, heard, targets, turn)
    message = repeat_sum(swap(message, "y", Y_ORDER))
    return final_part(src_index, row_index, swap(message, ("zh", "zl"), Z_ORDER), mask_param)


def solution(mesh):
    fine = Mesh(mesh.devices.reshape(2, 4, 2, 4, 8), ("zh", "x", "c", "zl", "y"))
    rows, src = ("zl", "y"), ("zh", "x", "c")
    placed = (P(rows, None), P(rows, src), P(), P(), P())
    return jax.shard_map(
        local, mesh=fine, in_specs=placed, out_specs=P(rows, src), check_vma=False
    )
```
